32 devices in a mesh: alpha: 4 (over y, core), beta: 8 (over z, x).
Axes of the slice: x: 2, y: 2, z: 4, core: 2. Of those that a mesh axis runs over, the one named last changes fastest.
Arguments:
- coeffs: float32 [8, 1024], P('alpha', 'beta'), may hold values from -6 to 6
- alpha_target: int32 [8, 132], P('alpha'), may hold values from 0 to 7
- alpha_pair: int32 [8, 132], P('alpha'), may hold values from 0 to 483
- alpha_sign: int32 [8, 132], P('alpha'), may hold values from -1 to 1
- beta_target: int32 [1024, 132], P('beta'), may hold values from 0 to 1023
- beta_pair: int32 [1024, 132], P('beta'), may hold values from 0 to 483
- beta_sign: int32 [1024, 132], P('beta'), may hold values from -1 to 1
- integrals: float32 [484, 484], replicated
- one_body: float32 [22, 22], replicated
Outputs:
- sigma: float32 [8, 1024], P('alpha', 'beta')
The draws below stay inside these ranges and needn't reach their ends.
All inputs are finite; a program needn't handle non-finite values.
Results may differ from the reference program's by a relative error of at most 0.0003.
Values sent between devices are 32-bit elements; how exact they have to be, the bound alone decides.
A program may use at most 64 MiB of HBM per device.

```python
import jax
import jax.numpy as jnp
from jax import lax

NORB = 22
SLOTS = 132
ROWB = 1
PAIRS = 484
NA = 8
NB = 1024


def draw_integrals(key, part):
    shape = (NORB, NORB, NORB, NORB)
    base = jax.random.normal(key, shape, jnp.float32)
    sym = base + jnp.transpose(base, (1, 0, 2, 3))
    sym = sym + jnp.transpose(sym, (0, 1, 3, 2))
    sym = sym + jnp.transpose(sym, (2, 3, 0, 1))
    return (sym * (2.8284271 / 8.0 / SLOTS)).reshape(NORB * NORB, NORB * NORB)


def draw_one_body(key, part):
    base = jax.random.normal(key, (NORB, NORB), jnp.float32)
    return (base + base.T) * (0.05 / 1.4142136)


def touch_ends(entries, own_key, smallest, high):
    longest = entries.shape.index(max(entries.shape))
    spots = []
    for shift in (0, 1):
        where = [jax.random.randint(jax.random.fold_in(own_key, axis), (), 0, length) for axis, length in enumerate(entries.shape)]
        where[longest] = (where[longest] + shift) % entries.shape[longest]
        spots.append(tuple(where))
    return entries.at[spots[0]].set(smallest).at[spots[1]].set(high)


def level_of(own_key, dims, cuts, smallest, largest):
    loudness = 1.0
    for position, parts in cuts:
        heights = jax.random.uniform(jax.random.fold_in(jax.random.fold_in(own_key, 6), position), (parts,), jnp.float32, smallest / len(cuts), largest / len(cuts))
        loudness = loudness * jnp.repeat(jnp.exp(heights), dims[position] // parts).reshape((-1,) + (1,) * (len(dims) - 1 - position))
    return loudness


def bell_draw(rng, extent, scale, reach, pieces=(), kind=jnp.bfloat16):
    loudness = level_of(rng, extent, pieces, -0.22, 0.18) if pieces else 1.0
    values = jax.random.normal(rng, extent, jnp.float32) * scale * loudness
    return jnp.minimum(jnp.maximum(values, -reach), reach).astype(kind)


def setup_inputs(seed: int = 0) -> dict:
    key_list = jax.random.split(jax.random.key(seed), 10)
    return {
        "coeffs": bell_draw(key_list[0], (NA, NB), 1.0, 6.0, ((0, 4), (1, 8)), jnp.float32),
        "alpha_target": touch_ends(jax.random.randint(key_list[1], (NA, SLOTS), 0, NA), jax.random.fold_in(key_list[1], 1), 0, NA - 1).astype(jnp.int32),
        "alpha_pair": touch_ends(jax.random.randint(key_list[2], (NA, SLOTS), 0, PAIRS), jax.random.fold_in(key_list[2], 1), 0, PAIRS - 1).astype(jnp.int32),
        "alpha_sign": touch_ends(jax.random.randint(key_list[3], (NA, SLOTS), -1, 2), jax.random.fold_in(key_list[3], 1), -1, 1).astype(jnp.int32),
        "beta_target": touch_ends(jax.random.randint(key_list[4], (NB, SLOTS), 0, NB), jax.random.fold_in(key_list[4], 1), 0, NB - 1).astype(jnp.int32),
        "beta_pair": touch_ends(jax.random.randint(key_list[5], (NB, SLOTS), 0, PAIRS), jax.random.fold_in(key_list[5], 1), 0, PAIRS - 1).astype(jnp.int32),
        "beta_sign": touch_ends(jax.random.randint(key_list[6], (NB, SLOTS), -1, 2), jax.random.fold_in(key_list[6], 1), -1, 1).astype(jnp.int32),
        "integrals": draw_integrals(jax.random.fold_in(key_list[9], 71), 0),
        "one_body": draw_one_body(jax.random.fold_in(key_list[9], 71), 0),
    }


def reference(coeffs, alpha_target, alpha_pair, alpha_sign, beta_target, beta_pair, beta_sign, integrals, one_body):
    highest = lax.Precision.HIGHEST
    h_flat = one_body.reshape(PAIRS)
    pair_ids = jnp.arange(PAIRS, dtype=jnp.int32)
    swapped = ((beta_pair % NORB) * NORB + beta_pair // NORB).astype(jnp.int32)
    beta_cols = jnp.arange(NB, dtype=jnp.int32)[:, None]
    beta_phase = beta_sign.astype(jnp.float32)
    flat_target = beta_target.reshape(NB * SLOTS)

    def one_block(inputs):
        targets, pairs, signs, c_rows = inputs
        gathered = coeffs[targets]
        picks = (pairs[:, :, None] == pair_ids[None, None, :]).astype(jnp.float32) * signs.astype(jnp.float32)[:, :, None]
        dens = jnp.einsum("isp,isb->ipb", picks, gathered, precision=highest)
        fock = jnp.einsum("pq,ipb->iqb", integrals, dens, precision=highest) + h_flat[None, :, None] * c_rows[:, None, :]
        local = jnp.einsum("p,ipb->ib", h_flat, dens, precision=highest)
        values = fock[:, swapped, beta_cols] * beta_phase[None, :, :]
        spread = jax.ops.segment_sum(values.reshape(ROWB, NB * SLOTS).T, flat_target, num_segments=NB)
        return local + spread.T

    blocks = NA // ROWB
    result = lax.map(one_block, (alpha_target.reshape(blocks, ROWB, SLOTS), alpha_pair.reshape(blocks, ROWB, SLOTS), alpha_sign.reshape(blocks, ROWB, SLOTS), coeffs.reshape(blocks, ROWB, NB)))
    return result.reshape(NA, NB)
```

```python
import functools

import jax
import jax.numpy as jnp
from jax import lax
from jax.experimental import pallas as pl
from jax.experimental.pallas import tpu as pltpu
from jax.sharding import PartitionSpec as P

MESH = pl.DeviceIdType.MESH
LANES = 128
NT = (((1,), (1,)), ((), ()))
NN = (((1,), (0,)), ((), ()))


def dot(a, b, dims=NN):
    return lax.dot_general(a, b, dims, preferred_element_type=jnp.float32)


def split(x):
    top = x.astype(jnp.bfloat16).astype(jnp.float32)
    return top, x - top


def divider(n, limit):
    s = 16
    m = (1 << s) // n + 1
    assert all((x * m) >> s == x // n for x in range(limit)) and limit * m < 2**31
    return m, s


def lane_pick(table, lane, chunk):
    out = None
    for i in range(table.shape[1] // LANES):
        part = jnp.take_along_axis(
            table[:, i * LANES : (i + 1) * LANES], lane, axis=1, mode="promise_in_bounds"
        )
        out = part if out is None else jnp.where(chunk == i, part, out)
    return out


def kernel(
    na,
    nb,
    build_rows,
    step_rows,
    coeffs,
    a_target,
    a_pair,
    a_sign,
    b_target,
    b_pair,
    b_sign,
    integrals,
    one_body,
    out,
    c_v,
    at_v,
    ap_v,
    as_v,
    bt_v,
    bp_v,
    bs_v,
    int_v,
    ob_v,
    slab,
    g_v,
    owner_v,
    lo_v,
    vals,
    hot,
    send,
    recv,
    load_sem,
    ag_send,
    ag_recv,
    rs_send,
    rs_recv,
):
    rows, cols = coeffs.shape
    slots = a_target.shape[1]
    norb = one_body.shape[0]
    npairs = norb * norb
    wide = g_v.shape[1]
    alphas = na * rows
    me_a = lax.axis_index("alpha")
    me_b = lax.axis_index("beta")
    f32, bf16 = jnp.float32, jnp.bfloat16

    loads = [
        pltpu.make_async_copy(src, dst, load_sem.at[i])
        for i, (src, dst) in enumerate(
            (
                (coeffs, c_v),
                (a_target, at_v),
                (a_pair, ap_v),
                (a_sign, as_v),
                (one_body, ob_v),
                (integrals, int_v),
                (b_target, bt_v),
                (b_pair, bp_v),
                (b_sign, bs_v),
            )
        )
    ]
    for load in loads:
        load.start()
    barrier = pltpu.get_barrier_semaphore()
    for k in range(1, na):
        pl.semaphore_signal(barrier, inc=1, device_id=(lax.rem(me_a + k, na), me_b), device_id_type=MESH)
    for k in range(1, nb):
        pl.semaphore_signal(barrier, inc=1, device_id=(me_a, lax.rem(me_b + k, nb)), device_id_type=MESH)
    loads[0].wait()
    pl.semaphore_wait(barrier, na + nb - 2)

    gathers = []
    for k in range(1, na):
        copy = pltpu.make_async_remote_copy(
            src_ref=c_v,
            dst_ref=slab.at[me_a],
            send_sem=ag_send.at[k - 1],
            recv_sem=ag_recv.at[k - 1],
            device_id=(lax.rem(me_a + k, na), me_b),
            device_id_type=MESH,
        )
        copy.start()
        gathers.append(copy)

    for i in range(1, 6):
        loads[i].wait()
    pair_ids = lax.broadcasted_iota(jnp.int32, (wide, slots), 0)
    string_ids = lax.broadcasted_iota(jnp.int32, (alphas, slots), 0)
    counts = []
    for a in range(rows):
        hits = jnp.where(pair_ids == ap_v[a : a + 1, :], 1.0, 0.0).astype(bf16)
        reach = jnp.where(string_ids == at_v[a : a + 1, :], as_v[a : a + 1, :].astype(f32), 0.0)
        counts.append(dot(reach.astype(bf16), hits, NT))
    counts = jnp.concatenate(counts, axis=0)
    mul, shift = divider(norb, wide)
    q = lax.broadcasted_iota(jnp.int32, (norb, wide), 1)
    q_row = (q * mul) >> shift
    q_col = q - q_row * norb
    orbital = lax.broadcasted_iota(jnp.int32, (norb, wide), 0)
    spread_h = lax.dot_general(
        ob_v[...],
        jnp.where(q_col == orbital, 1.0, 0.0),
        NN,
        precision=lax.Precision.HIGHEST,
        preferred_element_type=f32,
    )
    h = jnp.sum(jnp.where(q_row == orbital, spread_h, 0.0), axis=0, keepdims=True)
    weight = jnp.sum(counts * h, axis=1, keepdims=True)
    exact = counts[:, :npairs].astype(bf16)
    int_top, int_rest = split(int_v[...])
    g_v[...] = jnp.zeros_like(g_v)
    g_v[:, :npairs] = dot(exact, int_top.astype(bf16)) + dot(exact, int_rest.astype(bf16))
    line = lax.broadcasted_iota(jnp.int32, (rows * alphas, wide), 0)
    own = line == me_a * rows
    for a in range(1, rows):
        own = own | (line == a * alphas + me_a * rows + a)
    g = g_v[...] + jnp.where(own, h, 0.0)

    full, rem = slots // LANES, slots % LANES
    for i in range(6, 9):
        loads[i].wait()
    pair_bits = (wide - 1).bit_length()
    column_bits = (cols - 1).bit_length()

    def swap(pair):
        row = (pair * mul) >> shift
        return (pair - row * norb) * norb + row

    def pack(lower, upper):
        swapped = swap(bp_v[lower:upper, :])
        return (bt_v[lower:upper, :] << (pair_bits + 2)) | (swapped << 2) | (bs_v[lower:upper, :] + 1)

    codes = [pack(i * LANES, (i + 1) * LANES).astype(f32).T.astype(jnp.int32) for i in range(full)]
    for i, code in enumerate(codes):
        target = code >> (pair_bits + 2)
        owner_v[i * cols : (i + 1) * cols, :] = (target >> column_bits).astype(f32)
        lo_v[i * cols : (i + 1) * cols, :] = (target & (cols - 1)).astype(f32)
    if rem:
        target = bt_v[full * LANES :, :]
        owner_v[full * cols : full * cols + rem, :] = (target >> column_bits).astype(f32)
        lo_v[full * cols : full * cols + rem, :] = (target & (cols - 1)).astype(f32)
        tail = pack(full * LANES, slots).astype(f32)
        tail = jnp.concatenate([tail] * rows + [jnp.zeros((LANES - rows * rem, cols), f32)], axis=0)
        codes.append(tail.T.astype(jnp.int32))
    swapped = [(code >> 2) & ((1 << pair_bits) - 1) for code in codes]
    signs = [((code & 3) - 1).astype(f32) for code in codes]
    lanes = [index & (LANES - 1) for index in swapped]
    pieces = [index >> (LANES.bit_length() - 1) for index in swapped]

    lo_ids = lax.broadcasted_iota(jnp.int32, (cols, LANES), 0).astype(f32).astype(bf16)
    items = slots * cols // LANES

    @pl.loop(0, items // build_rows)
    def _(i):
        for r in range(build_rows):
            row = i * build_rows + r
            wanted = jnp.broadcast_to(lo_v[pl.ds(row, 1), :].astype(bf16), (cols, LANES))
            match = jnp.where(lo_ids == wanted, jnp.ones((), bf16), jnp.zeros((), bf16))
            hot[:, pl.ds(pl.multiple_of(row * LANES, LANES), LANES)] = match

    for copy in gathers:
        copy.wait()
    slab[me_a] = c_v[...]
    c = jnp.concatenate([slab[i] for i in range(na)], axis=0)
    c_top, c_rest = split(c)
    lhs = jnp.concatenate([c_top, c_rest, c_top], axis=0).T.astype(bf16)
    local, focks = [], []
    for a in range(rows):
        local.append(jnp.sum(weight[a * alphas : (a + 1) * alphas] * c, axis=0, keepdims=True))
        g_top, g_rest = split(g[a * alphas : (a + 1) * alphas])
        focks.append(dot(lhs, jnp.concatenate([g_top, g_top, g_rest], axis=0).astype(bf16)))
    for i in range(full):
        for a in range(rows):
            top, rest = split(lane_pick(focks[a], lanes[i], pieces[i]) * signs[i])
            vals[a, i * cols : (i + 1) * cols, :] = top
            vals[rows + a, i * cols : (i + 1) * cols, :] = rest
    if rem:
        lane_ids = lax.broadcasted_iota(jnp.int32, (cols, LANES), 1)
        tail = lane_pick(focks[0], lanes[full], pieces[full])
        for a in range(1, rows):
            tail = jnp.where(lane_ids < a * rem, tail, lane_pick(focks[a], lanes[full], pieces[full]))
        top, rest = split((tail * signs[full]).T)
        for a in range(rows):
            vals[a, full * cols : full * cols + rem, :] = top[a * rem : (a + 1) * rem]
            vals[rows + a, full * cols : full * cols + rem, :] = rest[a * rem : (a + 1) * rem]

    owner_ids = lax.broadcasted_iota(jnp.int32, (nb, LANES), 0).astype(f32)

    def step(i, total):
        lhs = []
        for r in range(step_rows):
            row = i * step_rows + r
            match = owner_ids == owner_v[pl.ds(row, 1), :]
            lhs.append(
                jnp.concatenate([jnp.where(match, vals[m, pl.ds(row, 1), :], 0.0) for m in range(2 * rows)], axis=0)
            )
        lhs = jnp.concatenate(lhs, axis=1).astype(bf16)
        width = step_rows * LANES
        return total + dot(hot[:, pl.ds(pl.multiple_of(i * width, LANES), width)], lhs, NT)

    total = lax.fori_loop(0, items // step_rows, step, jnp.zeros((cols, 2 * rows * nb), f32))
    if total.shape[1] % LANES:
        total = jnp.concatenate([total, jnp.zeros((cols, -total.shape[1] % LANES), f32)], axis=1)
    total = total.T
    for a in range(rows):
        send[:, a, :] = total[a * nb : (a + 1) * nb] + total[(rows + a) * nb : (rows + a + 1) * nb]

    copies = []
    for k in range(1, nb):
        to = lax.rem(me_b + k, nb)
        copy = pltpu.make_async_remote_copy(
            src_ref=send.at[to],
            dst_ref=recv.at[k - 1],
            send_sem=rs_send.at[k - 1],
            recv_sem=rs_recv.at[k - 1],
            device_id=(me_a, to),
            device_id_type=MESH,
        )
        copy.start()
        copies.append(copy)
    result = jnp.concatenate(local, axis=0) + send[me_b]
    for copy in copies:
        copy.wait()
    for k in range(1, nb):
        result = result + recv[k - 1]
    out[...] = result


def solution(mesh):
    na, nb = mesh.shape["alpha"], mesh.shape["beta"]

    def per_device(coeffs, a_target, a_pair, a_sign, b_target, b_pair, b_sign, integrals, one_body):
        rows, cols = coeffs.shape
        slots = a_target.shape[1]
        norb = one_body.shape[0]
        wide = pl.cdiv(norb * norb, LANES) * LANES
        items = slots * cols // LANES
        build_rows = next(n for n in range(12, 0, -1) if items % n == 0)
        step_rows = items
        i32, f32 = jnp.int32, jnp.float32
        padded = pl.cdiv(items, 8) * 8
        return pl.pallas_call(
            functools.partial(kernel, na, nb, build_rows, step_rows),
            out_shape=pltpu.VMEM((rows, cols), f32),
            in_specs=[pl.BlockSpec(memory_space=pl.ANY)] * 9,
            out_specs=pl.BlockSpec(memory_space=pltpu.VMEM),
            scratch_shapes=[
                pltpu.VMEM(coeffs.shape, f32),
                pltpu.VMEM(a_target.shape, i32),
                pltpu.VMEM(a_pair.shape, i32),
                pltpu.VMEM(a_sign.shape, i32),
                pltpu.VMEM(b_target.shape[::-1], i32),
                pltpu.VMEM(b_pair.shape[::-1], i32),
                pltpu.VMEM(b_sign.shape[::-1], i32),
                pltpu.VMEM(integrals.shape, f32),
                pltpu.VMEM(one_body.shape, f32),
                pltpu.VMEM((na, rows, cols), f32),
                pltpu.VMEM((rows * na * rows, wide), f32),
                pltpu.VMEM((padded, LANES), f32),
                pltpu.VMEM((padded, LANES), f32),
                pltpu.VMEM((2 * rows, padded, LANES), f32),
                pltpu.VMEM((cols, items * LANES), jnp.bfloat16),
                pltpu.VMEM((nb, rows, cols), f32),
                pltpu.VMEM((nb - 1, rows, cols), f32),
                pltpu.SemaphoreType.DMA((9,)),
                pltpu.SemaphoreType.DMA((na - 1,)),
                pltpu.SemaphoreType.DMA((na - 1,)),
                pltpu.SemaphoreType.DMA((nb - 1,)),
                pltpu.SemaphoreType.DMA((nb - 1,)),
            ],
            compiler_params=pltpu.CompilerParams(collective_id=0, has_side_effects=True),
        )(coeffs, a_target, a_pair, a_sign, b_target.T, b_pair.T, b_sign.T, integrals, one_body)

    placed = (
        P("alpha", "beta"),
        P("alpha", None),
        P("alpha", None),
        P("alpha", None),
        P("beta", None),
        P("beta", None),
        P("beta", None),
        P(),
        P(),
    )
    return jax.shard_map(
        per_device, mesh=mesh, in_specs=placed, out_specs=P("alpha", "beta"), check_vma=False
    )
```

```python
import functools

import jax
import jax.numpy as jnp
from jax import lax
from jax.experimental import pallas as pl
from jax.experimental.pallas import tpu as pltpu
from jax.sharding import PartitionSpec as P

MESH = pl.DeviceIdType.MESH
LANES = 128
SUB = 8
NT = (((1,), (1,)), ((), ()))
NN = (((1,), (0,)), ((), ()))


def dot(a, b, dims=NN):
    return lax.dot_general(a, b, dims, preferred_element_type=jnp.float32)


def split(x):
    top = x.astype(jnp.bfloat16).astype(jnp.float32)
    return top, x - top


def divider(n, limit):
    s = 16
    m = (1 << s) // n + 1
    assert all((x * m) >> s == x // n for x in range(limit)) and limit * m < 2**31
    return m, s


def kernel(
    na,
    nb,
    low,
    coeffs,
    a_target,
    a_pair,
    a_sign,
    b_target,
    b_pair,
    b_sign,
    integrals,
    one_body,
    out,
    at_v,
    ap_v,
    as_v,
    bt_v,
    bp_v,
    bs_v,
    int_v,
    ob_v,
    slab,
    g_v,
    counts_v,
    high_v,
    low_v,
    picked,
    vals,
    hot,
    group,
    send,
    recv,
    load_sem,
    ag_send,
    ag_recv,
    rs_send,
    rs_recv,
    ready,
):
    rows, cols = coeffs.shape
    slots = a_target.shape[1]
    norb = one_body.shape[0]
    npairs = norb * norb
    wide = g_v.shape[1]
    alphas = na * rows
    parts = cols // low
    high = parts * nb
    me_a = lax.axis_index("alpha")
    me_b = lax.axis_index("beta")
    f32, bf16 = jnp.float32, jnp.bfloat16

    loads = [
        pltpu.make_async_copy(src, dst, load_sem.at[i])
        for i, (src, dst) in enumerate(
            (
                (a_target, at_v),
                (a_pair, ap_v),
                (a_sign, as_v),
                (b_target, bt_v),
                (one_body, ob_v),
                (b_pair, bp_v),
                (b_sign, bs_v),
                (integrals, int_v),
                (coeffs, slab.at[me_a]),
            )
        )
    ]
    for load in loads:
        load.start()
    barrier = pltpu.get_barrier_semaphore()
    for k in range(1, na):
        pl.semaphore_signal(barrier, inc=1, device_id=(lax.rem(me_a + k, na), me_b), device_id_type=MESH)

    @pl.loop(me_b + 1, nb)
    def _(peer):
        pl.semaphore_signal(barrier, inc=1, device_id=(me_a, peer), device_id_type=MESH)

    gathers = [
        pltpu.make_async_remote_copy(
            src_ref=coeffs,
            dst_ref=slab.at[me_a],
            send_sem=ag_send.at[k - 1],
            recv_sem=ag_recv.at[k - 1],
            device_id=(lax.rem(me_a + k, na), me_b),
            device_id_type=MESH,
        )
        for k in range(1, na)
    ]

    def meet():
        pl.semaphore_wait(barrier, na - 1 + me_b)
        for copy in gathers:
            copy.start()

        @pl.loop(0, me_b)
        def _(peer):
            pl.semaphore_signal(ready, inc=1, device_id=(me_a, peer), device_id_type=MESH)

    far = 2 * me_a >= na

    @pl.when(far)
    def _():
        meet()

    for i in range(4):
        loads[i].wait()
    pair_ids = lax.broadcasted_iota(jnp.int32, (wide, slots), 0)
    string_ids = lax.broadcasted_iota(jnp.int32, (alphas, slots), 0)
    for a in range(rows):
        hits = jnp.where(pair_ids == ap_v[a : a + 1, :], 1.0, 0.0).astype(bf16)
        reach = jnp.where(string_ids == at_v[a : a + 1, :], as_v[a : a + 1, :].astype(f32), 0.0)
        counts_v[a * alphas : (a + 1) * alphas, :] = dot(reach.astype(bf16), hits, NT)

    low_bits = (low - 1).bit_length()
    part_bits = (parts - 1).bit_length()
    target = bt_v[...]
    upper = target >> low_bits
    high_v[...] = ((upper & (parts - 1)) * nb + (upper >> part_bits)).astype(f32)
    low_v[...] = (target & (low - 1)).astype(f32)
    low_ids = lax.broadcasted_iota(jnp.int32, (low, LANES), 0).astype(f32).astype(bf16)
    high_ids = lax.broadcasted_iota(jnp.int32, (high, LANES), 0).astype(f32).astype(bf16)
    one, zero = jnp.ones((), bf16), jnp.zeros((), bf16)

    def spots(row):
        where = pl.ds(pl.multiple_of(row * LANES, LANES), LANES)
        wanted = jnp.broadcast_to(low_v[pl.ds(row, 1), :].astype(bf16), (low, LANES))
        hot[:, where] = jnp.where(low_ids == wanted, one, zero)
        wanted = jnp.broadcast_to(high_v[pl.ds(row, 1), :].astype(bf16), (high, LANES))
        group[:, where] = jnp.where(high_ids == wanted, one, zero)

    @pl.loop(0, slots // 4)
    def _(i):
        for r in range(4):
            spots(i * 4 + r)

    for row in range(slots // 4 * 4, slots):
        spots(row)

    @pl.when(jnp.logical_not(far))
    def _():
        meet()

    for i in range(4, 8):
        loads[i].wait()
    counts = counts_v[...]
    mul, shift = divider(norb, wide)
    q = lax.broadcasted_iota(jnp.int32, (norb, wide), 1)
    q_row = (q * mul) >> shift
    q_col = q - q_row * norb
    orbital = lax.broadcasted_iota(jnp.int32, (norb, wide), 0)
    spread_h = lax.dot_general(
        ob_v[...],
        jnp.where(q_col == orbital, 1.0, 0.0),
        NN,
        precision=lax.Precision.HIGHEST,
        preferred_element_type=f32,
    )
    h = jnp.sum(jnp.where(q_row == orbital, spread_h, 0.0), axis=0, keepdims=True)
    weight = jnp.sum(counts * h, axis=1, keepdims=True)
    exact = counts[:, :npairs].astype(bf16)
    int_top, int_rest = split(int_v[...])
    g_v[...] = jnp.zeros_like(g_v)
    g_v[:, :npairs] = dot(exact, int_top.astype(bf16)) + dot(exact, int_rest.astype(bf16))
    line = lax.broadcasted_iota(jnp.int32, (rows * alphas, wide), 0)
    own = line == me_a * rows
    for a in range(1, rows):
        own = own | (line == a * alphas + me_a * rows + a)
    g_v[...] = g_v[...] + jnp.where(own, h, 0.0)

    def pick(lower, count):
        here = pl.ds(lower, count)
        pair = bp_v[here, :]
        row = (pair * mul) >> shift
        swapped = (pair - row * norb) * norb + row
        lane = swapped & (LANES - 1)
        piece = swapped >> (LANES.bit_length() - 1)
        sign = bs_v[here, :].astype(f32)
        for r in range(rows * alphas):
            value = None
            for i in range(wide // LANES):
                table = jnp.broadcast_to(g_v[r : r + 1, i * LANES : (i + 1) * LANES], (count, LANES))
                found = jnp.take_along_axis(table, lane, axis=1, mode="promise_in_bounds")
                value = found if value is None else jnp.where(piece == i, found, value)
            picked[r, here, :] = value * sign

    blocks = slots // SUB
    several = next(n for n in (8, 3, 2, 1) if blocks % n == 0)

    @pl.loop(0, blocks // several)
    def _(i):
        for n in range(several):
            pick(pl.multiple_of((i * several + n) * SUB, SUB), SUB)

    if slots % SUB:
        pick(blocks * SUB, slots % SUB)

    loads[8].wait()
    for copy in gathers:
        copy.wait()
    c = jnp.concatenate([slab[i] for i in range(na)], axis=0)
    local = [jnp.sum(weight[a * alphas : (a + 1) * alphas] * c, axis=0, keepdims=True) for a in range(rows)]
    for lower in range(0, slots, SUB):
        upper = min(lower + SUB, slots)
        for a in range(rows):
            value = None
            for i in range(alphas):
                term = picked[a * alphas + i, lower:upper, :] * c[i : i + 1]
                value = term if value is None else value + term
            top, rest = split(value)
            vals[a, lower:upper, :] = top
            vals[rows + a, lower:upper, :] = rest

    def step(i, total):
        lhs = []
        for r in range(66):
            row = i * 66 + r
            match = group[:, pl.ds(pl.multiple_of(row * LANES, LANES), LANES)]
            lhs.append(
                jnp.concatenate(
                    [
                        match * jnp.broadcast_to(vals[m, pl.ds(row, 1), :], (high, LANES)).astype(bf16)
                        for m in range(2 * rows)
                    ],
                    axis=0,
                )
            )
        width = 66 * LANES
        part = hot[:, pl.ds(pl.multiple_of(i * width, LANES), width)]
        return total + dot(part, jnp.concatenate(lhs, axis=1), NT)

    total = lax.fori_loop(0, slots // 66, step, jnp.zeros((low, 2 * rows * high), f32))
    lines = 2 * rows * high
    if lines % LANES:
        total = jnp.concatenate([total, jnp.zeros((low, -lines % LANES), f32)], axis=1)
    total = total.T
    for a in range(rows):
        both = total[a * high : (a + 1) * high] + total[(rows + a) * high : (rows + a + 1) * high]
        send[:, a, :] = jnp.concatenate([both[i * nb : (i + 1) * nb] for i in range(parts)], axis=1)


    @pl.when(me_b < nb - 1)
    def _():
        pl.semaphore_wait(ready, nb - 1 - me_b)

    copies = []
    for k in range(1, nb):
        to = lax.rem(me_b + k, nb)
        copy = pltpu.make_async_remote_copy(
            src_ref=send.at[to],
            dst_ref=recv.at[k - 1],
            send_sem=rs_send.at[k - 1],
            recv_sem=rs_recv.at[k - 1],
            device_id=(me_a, to),
            device_id_type=MESH,
        )
        copy.start()
        copies.append(copy)
    result = jnp.concatenate(local, axis=0) + send[me_b]
    for copy in copies:
        copy.wait()
    for k in range(1, nb):
        result = result + recv[k - 1]
    out[...] = result


def solution(mesh):
    na, nb = mesh.shape["alpha"], mesh.shape["beta"]

    def per_device(coeffs, a_target, a_pair, a_sign, b_target, b_pair, b_sign, integrals, one_body):
        rows, cols = coeffs.shape
        slots = a_target.shape[1]
        norb = one_body.shape[0]
        wide = pl.cdiv(norb * norb, LANES) * LANES
        assert cols == LANES
        low = cols // 2
        high = nb * (cols // low)
        i32, f32, bf16 = jnp.int32, jnp.float32, jnp.bfloat16
        pairs = rows * na * rows
        return pl.pallas_call(
            functools.partial(kernel, na, nb, low),
            out_shape=pltpu.VMEM((rows, cols), f32),
            in_specs=[pl.BlockSpec(memory_space=pl.ANY)] * 9,
            out_specs=pl.BlockSpec(memory_space=pltpu.VMEM),
            scratch_shapes=[
                pltpu.VMEM(a_target.shape, i32),
                pltpu.VMEM(a_pair.shape, i32),
                pltpu.VMEM(a_sign.shape, i32),
                pltpu.VMEM(b_target.shape[::-1], i32),
                pltpu.VMEM(b_pair.shape[::-1], i32),
                pltpu.VMEM(b_sign.shape[::-1], i32),
                pltpu.VMEM(integrals.shape, f32),
                pltpu.VMEM(one_body.shape, f32),
                pltpu.VMEM((na, rows, cols), f32),
                pltpu.VMEM((pairs, wide), f32),
                pltpu.VMEM((pairs, wide), f32),
                pltpu.VMEM((slots, LANES), f32),
                pltpu.VMEM((slots, LANES), f32),
                pltpu.VMEM((pairs, slots, LANES), f32),
                pltpu.VMEM((2 * rows, slots, LANES), f32),
                pltpu.VMEM((low, slots * LANES), bf16),
                pltpu.VMEM((high, slots * LANES), bf16),
                pltpu.VMEM((nb, rows, cols), f32),
                pltpu.VMEM((nb - 1, rows, cols), f32),
                pltpu.SemaphoreType.DMA((9,)),
                pltpu.SemaphoreType.DMA((na - 1,)),
                pltpu.SemaphoreType.DMA((na - 1,)),
                pltpu.SemaphoreType.DMA((nb - 1,)),
                pltpu.SemaphoreType.DMA((nb - 1,)),
                pltpu.SemaphoreType.REGULAR,
            ],
            compiler_params=pltpu.CompilerParams(collective_id=0, has_side_effects=True),
        )(coeffs, a_target, a_pair, a_sign, b_target.T, b_pair.T, b_sign.T, integrals, one_body)

    placed = (
        P("alpha", "beta"),
        P("alpha", None),
        P("alpha", None),
        P("alpha", None),
        P("beta", None),
        P("beta", None),
        P("beta", None),
        P(),
        P(),
    )
    return jax.shard_map(
        per_device, mesh=mesh, in_specs=placed, out_specs=P("alpha", "beta"), check_vma=False
    )
```

```python
import functools

import jax
import jax.numpy as jnp
from jax import lax
from jax.experimental import pallas as pl
from jax.experimental.pallas import tpu as pltpu
from jax.sharding import PartitionSpec as P

MESH = pl.DeviceIdType.MESH
LANES = 128
SUB = 8
NT = (((1,), (1,)), ((), ()))
NN = (((1,), (0,)), ((), ()))


def dot(a, b, dims=NN):
    return lax.dot_general(a, b, dims, preferred_element_type=jnp.float32)


def split(x):
    top = x.astype(jnp.bfloat16).astype(jnp.float32)
    return top, x - top


def divider(n, limit):
    s = 16
    m = (1 << s) // n + 1
    assert all((x * m) >> s == x // n for x in range(limit)) and limit * m < 2**31
    return m, s


def kernel(
    na,
    nb,
    low,
    small,
    coeffs,
    a_target,
    a_pair,
    a_sign,
    b_target,
    b_pair,
    b_sign,
    integrals,
    one_body,
    out,
    at_v,
    ap_v,
    as_v,
    bt_v,
    bp_v,
    bs_v,
    int_v,
    ob_v,
    slab,
    g_v,
    counts_v,
    high_v,
    low_v,
    picked,
    vals,
    hot,
    group,
    first_v,
    small_v,
    small_hot,
    small_group,
    early,
    send,
    recv,
    load_sem,
    ag_send,
    ag_recv,
    rs_send,
    rs_recv,
    ready,
):
    rows, cols = coeffs.shape
    slots = a_target.shape[1]
    norb = one_body.shape[0]
    npairs = norb * norb
    wide = g_v.shape[1]
    alphas = na * rows
    parts = cols // low
    high = parts * nb
    me_a = lax.axis_index("alpha")
    me_b = lax.axis_index("beta")
    f32, bf16 = jnp.float32, jnp.bfloat16

    loads = [
        pltpu.make_async_copy(src, dst, load_sem.at[i])
        for i, (src, dst) in enumerate(
            (
                (coeffs, slab.at[me_a]),
                (a_target, at_v),
                (a_pair, ap_v),
                (a_sign, as_v),
                (b_target, bt_v),
                (one_body, ob_v),
                (b_pair, bp_v),
                (b_sign, bs_v),
                (integrals, int_v),
            )
        )
    ]
    barrier = pltpu.get_barrier_semaphore()
    for k in range(1, na):
        pl.semaphore_signal(barrier, inc=1, device_id=(lax.rem(me_a + k, na), me_b), device_id_type=MESH)

    @pl.loop(me_b + 1, nb)
    def _(peer):
        pl.semaphore_signal(barrier, inc=1, device_id=(me_a, peer), device_id_type=MESH)

    for load in loads:
        load.start()
    gathers = [
        pltpu.make_async_remote_copy(
            src_ref=slab.at[me_a],
            dst_ref=slab.at[me_a],
            send_sem=ag_send.at[k - 1],
            recv_sem=ag_recv.at[k - 1],
            device_id=(lax.rem(me_a + k, na), me_b),
            device_id_type=MESH,
        )
        for k in range(1, na)
    ]

    def meet():
        pl.semaphore_wait(barrier, na - 1 + me_b)
        loads[0].wait()
        for copy in gathers:
            copy.start()

        @pl.loop(0, me_b)
        def _(peer):
            pl.semaphore_signal(ready, inc=1, device_id=(me_a, peer), device_id_type=MESH)

    far = 2 * me_a >= na

    @pl.when(far)
    def _():
        meet()

    for i in range(1, 5):
        loads[i].wait()
    pair_ids = lax.broadcasted_iota(jnp.int32, (wide, slots), 0)
    string_ids = lax.broadcasted_iota(jnp.int32, (alphas, slots), 0)
    for a in range(rows):
        hits = jnp.where(pair_ids == ap_v[a : a + 1, :], 1.0, 0.0).astype(bf16)
        reach = jnp.where(string_ids == at_v[a : a + 1, :], as_v[a : a + 1, :].astype(f32), 0.0)
        counts_v[a * alphas : (a + 1) * alphas, :] = dot(reach.astype(bf16), hits, NT)

    low_bits = (low - 1).bit_length()
    part_bits = (parts - 1).bit_length()
    target = bt_v[...]
    upper = target >> low_bits
    high_v[...] = ((upper & (parts - 1)) * nb + (upper >> part_bits)).astype(f32)
    low_v[...] = (target & (low - 1)).astype(f32)
    low_ids = lax.broadcasted_iota(jnp.int32, (low, LANES), 0).astype(f32).astype(bf16)
    high_ids = lax.broadcasted_iota(jnp.int32, (high, LANES), 0).astype(f32).astype(bf16)
    one, zero = jnp.ones((), bf16), jnp.zeros((), bf16)
    sets = LANES // small
    small_bits = (small - 1).bit_length()
    first_v[...] = (target >> small_bits).astype(f32)
    small_v[...] = (target & (small - 1)).astype(f32)
    small_ids = lax.broadcasted_iota(jnp.int32, (small, LANES), 0).astype(f32).astype(bf16)
    set_ids = (lax.broadcasted_iota(jnp.int32, (2 * rows * sets, LANES), 0) & (sets - 1)).astype(f32).astype(bf16)

    def spots(row):
        where = pl.ds(pl.multiple_of(row * LANES, LANES), LANES)
        wanted = jnp.broadcast_to(low_v[pl.ds(row, 1), :].astype(bf16), (low, LANES))
        hot[:, where] = jnp.where(low_ids == wanted, one, zero)
        wanted = jnp.broadcast_to(high_v[pl.ds(row, 1), :].astype(bf16), (high, LANES))
        group[:, where] = jnp.where(high_ids == wanted, one, zero)
        wanted = jnp.broadcast_to(small_v[pl.ds(row, 1), :].astype(bf16), (small, LANES))
        small_hot[:, where] = jnp.where(small_ids == wanted, one, zero)
        wanted = jnp.broadcast_to(first_v[pl.ds(row, 1), :].astype(bf16), (2 * rows * sets, LANES))
        small_group[:, where] = jnp.where(set_ids == wanted, one, zero)

    @pl.loop(0, slots // 4)
    def _(i):
        for r in range(4):
            spots(i * 4 + r)

    for row in range(slots // 4 * 4, slots):
        spots(row)

    @pl.when(jnp.logical_not(far))
    def _():
        meet()

    for i in range(5, 9):
        loads[i].wait()
    counts = counts_v[...]
    mul, shift = divider(norb, wide)
    q = lax.broadcasted_iota(jnp.int32, (norb, wide), 1)
    q_row = (q * mul) >> shift
    q_col = q - q_row * norb
    orbital = lax.broadcasted_iota(jnp.int32, (norb, wide), 0)
    spread_h = lax.dot_general(
        ob_v[...],
        jnp.where(q_col == orbital, 1.0, 0.0),
        NN,
        precision=lax.Precision.HIGHEST,
        preferred_element_type=f32,
    )
    h = jnp.sum(jnp.where(q_row == orbital, spread_h, 0.0), axis=0, keepdims=True)
    weight = jnp.sum(counts * h, axis=1, keepdims=True)
    exact = counts[:, :npairs].astype(bf16)
    int_top, int_rest = split(int_v[...])
    g_v[...] = jnp.zeros_like(g_v)
    g_v[:, :npairs] = dot(exact, int_top.astype(bf16)) + dot(exact, int_rest.astype(bf16))
    line = lax.broadcasted_iota(jnp.int32, (rows * alphas, wide), 0)
    own = line == me_a * rows
    for a in range(1, rows):
        own = own | (line == a * alphas + me_a * rows + a)
    g_v[...] = g_v[...] + jnp.where(own, h, 0.0)

    def pick(lower, count):
        here = pl.ds(lower, count)
        pair = bp_v[here, :]
        row = (pair * mul) >> shift
        swapped = (pair - row * norb) * norb + row
        lane = swapped & (LANES - 1)
        piece = swapped >> (LANES.bit_length() - 1)
        sign = bs_v[here, :].astype(f32)
        for r in range(rows * alphas):
            value = None
            for i in range(wide // LANES):
                table = jnp.broadcast_to(g_v[r : r + 1, i * LANES : (i + 1) * LANES], (count, LANES))
                found = jnp.take_along_axis(table, lane, axis=1, mode="promise_in_bounds")
                value = found if value is None else jnp.where(piece == i, found, value)
            picked[r, here, :] = value * sign

    blocks = slots // SUB
    several = next(n for n in (16, 8, 3, 2, 1) if blocks % n == 0)

    @pl.loop(0, blocks // several)
    def _(i):
        for n in range(several):
            pick(pl.multiple_of((i * several + n) * SUB, SUB), SUB)

    if slots % SUB:
        pick(blocks * SUB, slots % SUB)

    for copy in gathers:
        copy.wait()
    c = jnp.concatenate([slab[i] for i in range(na)], axis=0)
    local = [jnp.sum(weight[a * alphas : (a + 1) * alphas] * c, axis=0, keepdims=True) for a in range(rows)]
    for lower in range(0, slots, SUB):
        upper = min(lower + SUB, slots)
        for a in range(rows):
            value = None
            for i in range(alphas):
                term = picked[a * alphas + i, lower:upper, :] * c[i : i + 1]
                value = term if value is None else value + term
            top, rest = split(value)
            vals[a, lower:upper, :] = top
            vals[rows + a, lower:upper, :] = rest

    def small_step(i, total):
        lhs = []
        for r in range(66):
            row = i * 66 + r
            match = small_group[:, pl.ds(pl.multiple_of(row * LANES, LANES), LANES)]
            value = [jnp.broadcast_to(vals[m, pl.ds(row, 1), :], (sets, LANES)) for m in range(2 * rows)]
            lhs.append(match * jnp.concatenate(value, axis=0).astype(bf16))
        width = 66 * LANES
        part = small_hot[:, pl.ds(pl.multiple_of(i * width, LANES), width)]
        return total + dot(jnp.concatenate(lhs, axis=1), part, NT)

    total = lax.fori_loop(0, slots // 66, small_step, jnp.zeros((2 * rows * sets, small), f32))
    both = total[: rows * sets] + total[rows * sets :]
    for a in range(rows):
        early[a : a + 1, :] = jnp.concatenate([both[a * sets + i : a * sets + i + 1] for i in range(sets)], axis=1)

    def pass_on(k, source):
        return pltpu.make_async_remote_copy(
            src_ref=source,
            dst_ref=recv.at[k - 1],
            send_sem=rs_send.at[k - 1],
            recv_sem=rs_recv.at[k - 1],
            device_id=(me_a, lax.rem(me_b + k, nb)),
            device_id_type=MESH,
        )

    @pl.when(me_b > 0)
    def _():
        pass_on(nb - me_b, early).start()

    def step(i, total):
        lhs = []
        for r in range(66):
            row = i * 66 + r
            match = group[:, pl.ds(pl.multiple_of(row * LANES, LANES), LANES)]
            lhs.append(
                jnp.concatenate(
                    [
                        match * jnp.broadcast_to(vals[m, pl.ds(row, 1), :], (high, LANES)).astype(bf16)
                        for m in range(2 * rows)
                    ],
                    axis=0,
                )
            )
        width = 66 * LANES
        part = hot[:, pl.ds(pl.multiple_of(i * width, LANES), width)]
        return total + dot(jnp.concatenate(lhs, axis=1), part, NT)

    total = lax.fori_loop(0, slots // 66, step, jnp.zeros((2 * rows * high, low), f32))
    for a in range(rows):
        both = total[a * high : (a + 1) * high] + total[(rows + a) * high : (rows + a + 1) * high]
        send[:, a, :] = jnp.concatenate([both[i * nb : (i + 1) * nb] for i in range(parts)], axis=1)


    @pl.when(me_b < nb - 1)
    def _():
        pl.semaphore_wait(ready, nb - 1 - me_b)

    for k in range(1, nb):
        to = lax.rem(me_b + k, nb)

        @pl.when(to > 0)
        def _():
            pass_on(k, send.at[to]).start()

    result = jnp.concatenate(local, axis=0) + send[me_b]
    for k in range(1, nb):
        pass_on(k, early).wait()
    for k in range(1, nb):
        result = result + recv[k - 1]
    out[...] = result


def solution(mesh):
    na, nb = mesh.shape["alpha"], mesh.shape["beta"]

    def per_device(coeffs, a_target, a_pair, a_sign, b_target, b_pair, b_sign, integrals, one_body):
        rows, cols = coeffs.shape
        slots = a_target.shape[1]
        norb = one_body.shape[0]
        wide = pl.cdiv(norb * norb, LANES) * LANES
        assert cols == LANES
        low = cols // 2
        small = cols // 4
        high = nb * (cols // low)
        i32, f32, bf16 = jnp.int32, jnp.float32, jnp.bfloat16
        pairs = rows * na * rows
        return pl.pallas_call(
            functools.partial(kernel, na, nb, low, small),
            out_shape=pltpu.VMEM((rows, cols), f32),
            in_specs=[pl.BlockSpec(memory_space=pl.ANY)] * 9,
            out_specs=pl.BlockSpec(memory_space=pltpu.VMEM),
            scratch_shapes=[
                pltpu.VMEM(a_target.shape, i32),
                pltpu.VMEM(a_pair.shape, i32),
                pltpu.VMEM(a_sign.shape, i32),
                pltpu.VMEM(b_target.shape[::-1], i32),
                pltpu.VMEM(b_pair.shape[::-1], i32),
                pltpu.VMEM(b_sign.shape[::-1], i32),
                pltpu.VMEM(integrals.shape, f32),
                pltpu.VMEM(one_body.shape, f32),
                pltpu.VMEM((na, rows, cols), f32),
                pltpu.VMEM((pairs, wide), f32),
                pltpu.VMEM((pairs, wide), f32),
                pltpu.VMEM((slots, LANES), f32),
                pltpu.VMEM((slots, LANES), f32),
                pltpu.VMEM((pairs, slots, LANES), f32),
                pltpu.VMEM((2 * rows, slots, LANES), f32),
                pltpu.VMEM((low, slots * LANES), bf16),
                pltpu.VMEM((high, slots * LANES), bf16),
                pltpu.VMEM((slots, LANES), f32),
                pltpu.VMEM((slots, LANES), f32),
                pltpu.VMEM((small, slots * LANES), bf16),
                pltpu.VMEM((2 * rows * (cols // small), slots * LANES), bf16),
                pltpu.VMEM((rows, cols), f32),
                pltpu.VMEM((nb, rows, cols), f32),
                pltpu.VMEM((nb - 1, rows, cols), f32),
                pltpu.SemaphoreType.DMA((9,)),
                pltpu.SemaphoreType.DMA((na - 1,)),
                pltpu.SemaphoreType.DMA((na - 1,)),
                pltpu.SemaphoreType.DMA((nb - 1,)),
                pltpu.SemaphoreType.DMA((nb - 1,)),
                pltpu.SemaphoreType.REGULAR,
            ],
            compiler_params=pltpu.CompilerParams(collective_id=0, has_side_effects=True),
        )(coeffs, a_target, a_pair, a_sign, b_target.T, b_pair.T, b_sign.T, integrals, one_body)

    placed = (
        P("alpha", "beta"),
        P("alpha", None),
        P("alpha", None),
        P("alpha", None),
        P("beta", None),
        P("beta", None),
        P("beta", None),
        P(),
        P(),
    )
    return jax.shard_map(
        per_device, mesh=mesh, in_specs=placed, out_specs=P("alpha", "beta"), check_vma=False
    )
```

```python
import functools

import jax
import jax.numpy as jnp
from jax import lax
from jax.experimental import pallas as pl
from jax.experimental.pallas import tpu as pltpu
from jax.sharding import PartitionSpec as P

MESH = pl.DeviceIdType.MESH
LANES = 128
SUB = 8
NT = (((1,), (1,)), ((), ()))
NN = (((1,), (0,)), ((), ()))


def dot(a, b, dims=NN):
    return lax.dot_general(a, b, dims, preferred_element_type=jnp.float32)


def split(x):
    top = x.astype(jnp.bfloat16).astype(jnp.float32)
    return top, x - top


def divider(n, limit):
    s = 16
    m = (1 << s) // n + 1
    assert all((x * m) >> s == x // n for x in range(limit)) and limit * m < 2**31
    return m, s


def kernel(
    na,
    nb,
    low,
    small,
    coeffs,
    a_target,
    a_pair,
    a_sign,
    b_target,
    b_pair,
    b_sign,
    integrals,
    one_body,
    out,
    at_v,
    ap_v,
    as_v,
    bt_v,
    bp_v,
    bs_v,
    int_v,
    ob_v,
    slab,
    g_v,
    counts_v,
    h_v,
    tot_v,
    high_v,
    low_v,
    picked,
    vals,
    hot,
    group,
    first_v,
    small_v,
    small_hot,
    small_group,
    early,
    send,
    recv,
    load_sem,
    ag_send,
    ag_recv,
    rs_send,
    rs_recv,
    ready,
):
    rows, cols = coeffs.shape
    slots = a_target.shape[1]
    norb = one_body.shape[0]
    npairs = norb * norb
    wide = g_v.shape[1]
    alphas = na * rows
    parts = cols // low
    high = parts * nb
    me_a = lax.axis_index("alpha")
    me_b = lax.axis_index("beta")
    f32, bf16 = jnp.float32, jnp.bfloat16

    loads = [
        pltpu.make_async_copy(src, dst, load_sem.at[i])
        for i, (src, dst) in enumerate(
            (
                (coeffs, slab.at[me_a]),
                (a_target, at_v),
                (a_pair, ap_v),
                (a_sign, as_v),
                (b_target, bt_v),
                (one_body, ob_v),
                (b_pair, bp_v),
                (b_sign, bs_v),
                (integrals, int_v),
            )
        )
    ]
    barrier = pltpu.get_barrier_semaphore()
    for k in range(1, na):
        pl.semaphore_signal(barrier, inc=1, device_id=(lax.rem(me_a + k, na), me_b), device_id_type=MESH)

    @pl.loop(me_b + 1, nb)
    def _(peer):
        pl.semaphore_signal(barrier, inc=1, device_id=(me_a, peer), device_id_type=MESH)

    for load in loads:
        load.start()
    gathers = [
        pltpu.make_async_remote_copy(
            src_ref=slab.at[me_a],
            dst_ref=slab.at[me_a],
            send_sem=ag_send.at[k - 1],
            recv_sem=ag_recv.at[k - 1],
            device_id=(lax.rem(me_a + k, na), me_b),
            device_id_type=MESH,
        )
        for k in range(1, na)
    ]

    def meet():
        pl.semaphore_wait(barrier, na - 1 + me_b)
        loads[0].wait()
        for copy in gathers:
            copy.start()

        @pl.loop(0, me_b)
        def _(peer):
            pl.semaphore_signal(ready, inc=1, device_id=(me_a, peer), device_id_type=MESH)

    far = 2 * me_a >= na

    @pl.when(far)
    def _():
        meet()

    sets = LANES // small
    few = next(n for n in range(12, 0, -1) if slots % n == 0)
    one, zero = jnp.ones((), bf16), jnp.zeros((), bf16)

    def prepare():
        for i in range(1, 5):
            loads[i].wait()
        pair_ids = lax.broadcasted_iota(jnp.int32, (wide, slots), 0)
        string_ids = lax.broadcasted_iota(jnp.int32, (alphas, slots), 0)
        for a in range(rows):
            hits = jnp.where(pair_ids == ap_v[a : a + 1, :], 1.0, 0.0).astype(bf16)
            reach = jnp.where(string_ids == at_v[a : a + 1, :], as_v[a : a + 1, :].astype(f32), 0.0)
            counts_v[a * alphas : (a + 1) * alphas, :] = dot(reach.astype(bf16), hits, NT)

        target = bt_v[...]
        one, zero = jnp.ones((), bf16), jnp.zeros((), bf16)
        sets = LANES // small
        small_bits = (small - 1).bit_length()
        first_v[...] = (target >> small_bits).astype(f32)
        small_v[...] = (target & (small - 1)).astype(f32)
        small_ids = lax.broadcasted_iota(jnp.int32, (small, LANES), 0).astype(f32).astype(bf16)
        set_ids = (lax.broadcasted_iota(jnp.int32, (2 * rows * sets, LANES), 0) & (sets - 1)).astype(f32).astype(bf16)

        def spots(row):
            where = pl.ds(pl.multiple_of(row * LANES, LANES), LANES)
            wanted = jnp.broadcast_to(small_v[pl.ds(row, 1), :].astype(bf16), (small, LANES))
            small_hot[:, where] = jnp.where(small_ids == wanted, one, zero)
            wanted = jnp.broadcast_to(first_v[pl.ds(row, 1), :].astype(bf16), (2 * rows * sets, LANES))
            small_group[:, where] = jnp.where(set_ids == wanted, one, zero)

        @pl.loop(0, slots // few)
        def _(i):
            for r in range(few):
                spots(i * few + r)

        @pl.when(jnp.logical_not(far))
        def _():
            meet()

        for i in range(5, 9):
            loads[i].wait()
        counts = counts_v[...]
        mul, shift = divider(norb, wide)
        q = lax.broadcasted_iota(jnp.int32, (norb, wide), 1)
        q_row = (q * mul) >> shift
        q_col = q - q_row * norb
        orbital = lax.broadcasted_iota(jnp.int32, (norb, wide), 0)
        spread_h = lax.dot_general(
            ob_v[...],
            jnp.where(q_col == orbital, 1.0, 0.0),
            NN,
            precision=lax.Precision.HIGHEST,
            preferred_element_type=f32,
        )
        h = jnp.sum(jnp.where(q_row == orbital, spread_h, 0.0), axis=0, keepdims=True)
        h_v[...] = h
        exact = counts[:, :npairs].astype(bf16)
        int_top, int_rest = split(int_v[...])
        g_v[...] = jnp.zeros_like(g_v)
        g_v[:, :npairs] = dot(exact, int_top.astype(bf16)) + dot(exact, int_rest.astype(bf16))
        line = lax.broadcasted_iota(jnp.int32, (rows * alphas, wide), 0)
        own = line == me_a * rows
        for a in range(1, rows):
            own = own | (line == a * alphas + me_a * rows + a)
        g_v[...] = g_v[...] + jnp.where(own, h, 0.0)

        def pick(lower, count):
            here = pl.ds(lower, count)
            pair = bp_v[here, :]
            row = (pair * mul) >> shift
            swapped = (pair - row * norb) * norb + row
            lane = swapped & (LANES - 1)
            piece = swapped >> (LANES.bit_length() - 1)
            sign = bs_v[here, :].astype(f32)
            for r in range(rows * alphas):
                value = None
                for i in range(wide // LANES):
                    table = jnp.broadcast_to(g_v[r : r + 1, i * LANES : (i + 1) * LANES], (count, LANES))
                    found = jnp.take_along_axis(table, lane, axis=1, mode="promise_in_bounds")
                    value = found if value is None else jnp.where(piece == i, found, value)
                picked[r, here, :] = value * sign

        blocks = slots // SUB
        several = next(n for n in (16, 8, 3, 2, 1) if blocks % n == 0)

        @pl.loop(0, blocks // several)
        def _(i):
            for n in range(several):
                pick(pl.multiple_of((i * several + n) * SUB, SUB), SUB)

        if slots % SUB:
            pick(blocks * SUB, slots % SUB)

        for copy in gathers:
            copy.wait()
        c = jnp.concatenate([slab[i] for i in range(na)], axis=0)
        for lower in range(0, slots, SUB):
            upper = min(lower + SUB, slots)
            for a in range(rows):
                value = None
                for i in range(alphas):
                    term = picked[a * alphas + i, lower:upper, :] * c[i : i + 1]
                    value = term if value is None else value + term
                top, rest = split(value)
                vals[a, lower:upper, :] = top
                vals[rows + a, lower:upper, :] = rest


    @pl.loop(0, 2)
    def _(i):
        @pl.when(i == 1)
        def _():
            prepare()

        lhs = []
        for row in range(slots):
            match = small_group[:, row * LANES : (row + 1) * LANES]
            value = [jnp.broadcast_to(vals[m, row : row + 1, :], (sets, LANES)) for m in range(2 * rows)]
            lhs.append(match * jnp.concatenate(value, axis=0).astype(bf16))
        tot_v[...] = dot(jnp.concatenate(lhs, axis=1), small_hot[...], NT)

    total = tot_v[...]
    both = total[: rows * sets] + total[rows * sets :]
    for a in range(rows):
        early[a : a + 1, :] = jnp.concatenate([both[a * sets + i : a * sets + i + 1] for i in range(sets)], axis=1)

    def pass_on(k, source):
        return pltpu.make_async_remote_copy(
            src_ref=source,
            dst_ref=recv.at[k - 1],
            send_sem=rs_send.at[k - 1],
            recv_sem=rs_recv.at[k - 1],
            device_id=(me_a, lax.rem(me_b + k, nb)),
            device_id_type=MESH,
        )

    @pl.when(me_b > 0)
    def _():
        pass_on(nb - me_b, early).start()

    low_bits = (low - 1).bit_length()
    part_bits = (parts - 1).bit_length()
    target = bt_v[...]
    upper = target >> low_bits
    high_v[...] = ((upper & (parts - 1)) * nb + (upper >> part_bits)).astype(f32)
    low_v[...] = (target & (low - 1)).astype(f32)
    low_ids = lax.broadcasted_iota(jnp.int32, (low, LANES), 0).astype(f32).astype(bf16)
    high_ids = lax.broadcasted_iota(jnp.int32, (high, LANES), 0).astype(f32).astype(bf16)
    one, zero = jnp.ones((), bf16), jnp.zeros((), bf16)

    @pl.loop(0, slots // few)
    def _(i):
        for r in range(few):
            row = i * few + r
            where = pl.ds(pl.multiple_of(row * LANES, LANES), LANES)
            wanted = jnp.broadcast_to(low_v[pl.ds(row, 1), :].astype(bf16), (low, LANES))
            hot[:, where] = jnp.where(low_ids == wanted, one, zero)
            wanted = jnp.broadcast_to(high_v[pl.ds(row, 1), :].astype(bf16), (high, LANES))
            group[:, where] = jnp.where(high_ids == wanted, one, zero)

    turn = slots // 2 if slots % 2 == 0 else slots

    def step(i, total):
        lhs = []
        for r in range(turn):
            row = i * turn + r
            match = group[:, pl.ds(pl.multiple_of(row * LANES, LANES), LANES)]
            lhs.append(
                jnp.concatenate(
                    [
                        match * jnp.broadcast_to(vals[m, pl.ds(row, 1), :], (high, LANES)).astype(bf16)
                        for m in range(2 * rows)
                    ],
                    axis=0,
                )
            )
        width = turn * LANES
        part = hot[:, pl.ds(pl.multiple_of(i * width, LANES), width)]
        return total + dot(jnp.concatenate(lhs, axis=1), part, NT)

    total = lax.fori_loop(0, slots // turn, step, jnp.zeros((2 * rows * high, low), f32))
    for a in range(rows):
        both = total[a * high : (a + 1) * high] + total[(rows + a) * high : (rows + a + 1) * high]
        send[:, a, :] = jnp.concatenate([both[i * nb : (i + 1) * nb] for i in range(parts)], axis=1)


    @pl.when(me_b < nb - 1)
    def _():
        pl.semaphore_wait(ready, nb - 1 - me_b)

    for k in range(1, nb):
        to = lax.rem(me_b + k, nb)

        @pl.when(to > 0)
        def _():
            pass_on(k, send.at[to]).start()

    weight = jnp.sum(counts_v[...] * h_v[...], axis=1, keepdims=True)
    c = jnp.concatenate([slab[i] for i in range(na)], axis=0)
    local = [jnp.sum(weight[a * alphas : (a + 1) * alphas] * c, axis=0, keepdims=True) for a in range(rows)]
    result = jnp.concatenate(local, axis=0) + send[me_b]
    for k in range(1, nb):
        pass_on(k, early).wait()
    for k in range(1, nb):
        result = result + recv[k - 1]
    out[...] = result


def solution(mesh):
    na, nb = mesh.shape["alpha"], mesh.shape["beta"]

    def per_device(coeffs, a_target, a_pair, a_sign, b_target, b_pair, b_sign, integrals, one_body):
        rows, cols = coeffs.shape
        slots = a_target.shape[1]
        norb = one_body.shape[0]
        wide = pl.cdiv(norb * norb, LANES) * LANES
        assert cols == LANES
        low = cols // 2
        small = cols // 4
        high = nb * (cols // low)
        i32, f32, bf16 = jnp.int32, jnp.float32, jnp.bfloat16
        pairs = rows * na * rows
        return pl.pallas_call(
            functools.partial(kernel, na, nb, low, small),
            out_shape=pltpu.VMEM((rows, cols), f32),
            in_specs=[pl.BlockSpec(memory_space=pl.ANY)] * 9,
            out_specs=pl.BlockSpec(memory_space=pltpu.VMEM),
            scratch_shapes=[
                pltpu.VMEM(a_target.shape, i32),
                pltpu.VMEM(a_pair.shape, i32),
                pltpu.VMEM(a_sign.shape, i32),
                pltpu.VMEM(b_target.shape[::-1], i32),
                pltpu.VMEM(b_pair.shape[::-1], i32),
                pltpu.VMEM(b_sign.shape[::-1], i32),
                pltpu.VMEM(integrals.shape, f32),
                pltpu.VMEM(one_body.shape, f32),
                pltpu.VMEM((na, rows, cols), f32),
                pltpu.VMEM((pairs, wide), f32),
                pltpu.VMEM((pairs, wide), f32),
                pltpu.VMEM((1, wide), f32),
                pltpu.VMEM((2 * rows * (cols // small), small), f32),
                pltpu.VMEM((slots, LANES), f32),
                pltpu.VMEM((slots, LANES), f32),
                pltpu.VMEM((pairs, slots, LANES), f32),
                pltpu.VMEM((2 * rows, slots, LANES), f32),
                pltpu.VMEM((low, slots * LANES), bf16),
                pltpu.VMEM((high, slots * LANES), bf16),
                pltpu.VMEM((slots, LANES), f32),
                pltpu.VMEM((slots, LANES), f32),
                pltpu.VMEM((small, slots * LANES), bf16),
                pltpu.VMEM((2 * rows * (cols // small), slots * LANES), bf16),
                pltpu.VMEM((rows, cols), f32),
                pltpu.VMEM((nb, rows, cols), f32),
                pltpu.VMEM((nb - 1, rows, cols), f32),
                pltpu.SemaphoreType.DMA((9,)),
                pltpu.SemaphoreType.DMA((na - 1,)),
                pltpu.SemaphoreType.DMA((na - 1,)),
                pltpu.SemaphoreType.DMA((nb - 1,)),
                pltpu.SemaphoreType.DMA((nb - 1,)),
                pltpu.SemaphoreType.REGULAR,
            ],
            compiler_params=pltpu.CompilerParams(collective_id=0, has_side_effects=True),
        )(coeffs, a_target, a_pair, a_sign, b_target.T, b_pair.T, b_sign.T, integrals, one_body)

    placed = (
        P("alpha", "beta"),
        P("alpha", None),
        P("alpha", None),
        P("alpha", None),
        P("beta", None),
        P("beta", None),
        P("beta", None),
        P(),
        P(),
    )
    return jax.shard_map(
        per_device, mesh=mesh, in_specs=placed, out_specs=P("alpha", "beta"), check_vma=False
    )
```

```python
import functools

import jax
import jax.numpy as jnp
from jax import lax
from jax.experimental import pallas as pl
from jax.experimental.pallas import tpu as pltpu
from jax.sharding import PartitionSpec as P

MESH = pl.DeviceIdType.MESH
LANES = 128
SUB = 8
NT = (((1,), (1,)), ((), ()))
NN = (((1,), (0,)), ((), ()))


def dot(a, b, dims=NN):
    return lax.dot_general(a, b, dims, preferred_element_type=jnp.float32)


def split(x):
    top = x.astype(jnp.bfloat16).astype(jnp.float32)
    return top, x - top


def divider(n, limit):
    s = 16
    m = (1 << s) // n + 1
    assert all((x * m) >> s == x // n for x in range(limit)) and limit * m < 2**31
    return m, s


def kernel(
    na,
    nb,
    low,
    small,
    coeffs,
    a_target,
    a_pair,
    a_sign,
    b_target,
    b_pair,
    b_sign,
    integrals,
    one_body,
    out,
    at_v,
    ap_v,
    as_v,
    bt_v,
    bp_v,
    bs_v,
    int_v,
    ob_v,
    slab,
    g_v,
    counts_v,
    h_v,
    high_v,
    low_v,
    picked,
    vals,
    hot,
    group,
    first_v,
    small_v,
    small_hot,
    small_group,
    early,
    send,
    recv,
    load_sem,
    ag_send,
    ag_recv,
    rs_send,
    rs_recv,
    ready,
):
    rows, cols = coeffs.shape
    slots = a_target.shape[1]
    norb = one_body.shape[0]
    npairs = norb * norb
    wide = g_v.shape[1]
    alphas = na * rows
    parts = cols // low
    high = parts * nb
    me_a = lax.axis_index("alpha")
    me_b = lax.axis_index("beta")
    f32, bf16 = jnp.float32, jnp.bfloat16

    loads = [
        pltpu.make_async_copy(src, dst, load_sem.at[i])
        for i, (src, dst) in enumerate(
            (
                (coeffs, slab.at[me_a]),
                (a_target, at_v),
                (a_pair, ap_v),
                (a_sign, as_v),
                (b_target, bt_v),
                (one_body, ob_v),
                (b_pair, bp_v),
                (b_sign, bs_v),
                (integrals, int_v),
            )
        )
    ]
    barrier = pltpu.get_barrier_semaphore()
    for k in range(1, na):
        pl.semaphore_signal(barrier, inc=1, device_id=(lax.rem(me_a + k, na), me_b), device_id_type=MESH)

    @pl.loop(me_b + 1, nb)
    def _(peer):
        pl.semaphore_signal(barrier, inc=1, device_id=(me_a, peer), device_id_type=MESH)

    for load in loads:
        load.start()
    gathers = [
        pltpu.make_async_remote_copy(
            src_ref=slab.at[me_a],
            dst_ref=slab.at[me_a],
            send_sem=ag_send.at[k - 1],
            recv_sem=ag_recv.at[k - 1],
            device_id=(lax.rem(me_a + k, na), me_b),
            device_id_type=MESH,
        )
        for k in range(1, na)
    ]

    def meet():
        pl.semaphore_wait(barrier, na - 1 + me_b)
        loads[0].wait()
        for copy in gathers:
            copy.start()

        @pl.loop(0, me_b)
        def _(peer):
            pl.semaphore_signal(ready, inc=1, device_id=(me_a, peer), device_id_type=MESH)

    far = 2 * me_a >= na

    @pl.when(far)
    def _():
        meet()

    sets = LANES // small
    few = next(n for n in range(12, 0, -1) if slots % n == 0)
    one, zero = jnp.ones((), bf16), jnp.zeros((), bf16)

    def prepare():
        for i in range(1, 5):
            loads[i].wait()
        pair_ids = lax.broadcasted_iota(jnp.int32, (wide, slots), 0)
        string_ids = lax.broadcasted_iota(jnp.int32, (alphas, slots), 0)
        for a in range(rows):
            hits = jnp.where(pair_ids == ap_v[a : a + 1, :], 1.0, 0.0).astype(bf16)
            reach = jnp.where(string_ids == at_v[a : a + 1, :], as_v[a : a + 1, :].astype(f32), 0.0)
            counts_v[a * alphas : (a + 1) * alphas, :] = dot(reach.astype(bf16), hits, NT)

        target = bt_v[...]
        one, zero = jnp.ones((), bf16), jnp.zeros((), bf16)
        sets = LANES // small
        small_bits = (small - 1).bit_length()
        first_v[...] = (target >> small_bits).astype(f32)
        small_v[...] = (target & (small - 1)).astype(f32)
        small_ids = lax.broadcasted_iota(jnp.int32, (small, LANES), 0).astype(f32).astype(bf16)
        set_ids = (lax.broadcasted_iota(jnp.int32, (2 * rows * sets, LANES), 0) & (sets - 1)).astype(f32).astype(bf16)

        def spots(row):
            where = pl.ds(pl.multiple_of(row * LANES, LANES), LANES)
            wanted = jnp.broadcast_to(small_v[pl.ds(row, 1), :].astype(bf16), (small, LANES))
            small_hot[:, where] = jnp.where(small_ids == wanted, one, zero)
            wanted = jnp.broadcast_to(first_v[pl.ds(row, 1), :].astype(bf16), (2 * rows * sets, LANES))
            small_group[:, where] = jnp.where(set_ids == wanted, one, zero)

        @pl.loop(0, slots // few)
        def _(i):
            for r in range(few):
                spots(i * few + r)

        @pl.when(jnp.logical_not(far))
        def _():
            meet()

        for i in range(5, 9):
            loads[i].wait()
        counts = counts_v[...]
        mul, shift = divider(norb, wide)
        q = lax.broadcasted_iota(jnp.int32, (norb, wide), 1)
        q_row = (q * mul) >> shift
        q_col = q - q_row * norb
        orbital = lax.broadcasted_iota(jnp.int32, (norb, wide), 0)
        spread_h = lax.dot_general(
            ob_v[...],
            jnp.where(q_col == orbital, 1.0, 0.0),
            NN,
            precision=lax.Precision.HIGHEST,
            preferred_element_type=f32,
        )
        h = jnp.sum(jnp.where(q_row == orbital, spread_h, 0.0), axis=0, keepdims=True)
        h_v[...] = h
        exact = counts[:, :npairs].astype(bf16)
        int_top, int_rest = split(int_v[...])
        g_v[...] = jnp.zeros_like(g_v)
        g_v[:, :npairs] = dot(exact, int_top.astype(bf16)) + dot(exact, int_rest.astype(bf16))
        line = lax.broadcasted_iota(jnp.int32, (rows * alphas, wide), 0)
        own = line == me_a * rows
        for a in range(1, rows):
            own = own | (line == a * alphas + me_a * rows + a)
        g_v[...] = g_v[...] + jnp.where(own, h, 0.0)

        def pick(lower, count):
            here = pl.ds(lower, count)
            pair = bp_v[here, :]
            row = (pair * mul) >> shift
            swapped = (pair - row * norb) * norb + row
            lane = swapped & (LANES - 1)
            piece = swapped >> (LANES.bit_length() - 1)
            sign = bs_v[here, :].astype(f32)
            for r in range(rows * alphas):
                value = None
                for i in range(wide // LANES):
                    table = jnp.broadcast_to(g_v[r : r + 1, i * LANES : (i + 1) * LANES], (count, LANES))
                    found = jnp.take_along_axis(table, lane, axis=1, mode="promise_in_bounds")
                    value = found if value is None else jnp.where(piece == i, found, value)
                picked[r, here, :] = value * sign

        blocks = slots // SUB
        several = next(n for n in (16, 8, 3, 2, 1) if blocks % n == 0)

        @pl.loop(0, blocks // several)
        def _(i):
            for n in range(several):
                pick(pl.multiple_of((i * several + n) * SUB, SUB), SUB)

        if slots % SUB:
            pick(blocks * SUB, slots % SUB)

        for k in sorted(range(1, na), key=lambda k: k == na // 2):
            gathers[k - 1].wait_recv()
        c = jnp.concatenate([slab[i] for i in range(na)], axis=0)
        for lower in range(0, slots, SUB):
            upper = min(lower + SUB, slots)
            for a in range(rows):
                value = None
                for i in range(alphas):
                    term = picked[a * alphas + i, lower:upper, :] * c[i : i + 1]
                    value = term if value is None else value + term
                top, rest = split(value)
                vals[a, lower:upper, :] = top
                vals[rows + a, lower:upper, :] = rest


    @pl.loop(0, 2)
    def _(i):
        @pl.when(i == 1)
        def _():
            prepare()

        lhs = []
        for row in range(slots):
            match = small_group[:, row * LANES : (row + 1) * LANES]
            value = [jnp.broadcast_to(vals[m, row : row + 1, :], (sets, LANES)) for m in range(2 * rows)]
            lhs.append(match * jnp.concatenate(value, axis=0).astype(bf16))
        total = dot(jnp.concatenate(lhs, axis=1), small_hot[...], NT)
        both = total[: rows * sets] + total[rows * sets :]
        for a in range(rows):
            early[a : a + 1, :] = jnp.concatenate([both[a * sets + n : a * sets + n + 1] for n in range(sets)], axis=1)

    def pass_on(k, source):
        return pltpu.make_async_remote_copy(
            src_ref=source,
            dst_ref=recv.at[k - 1],
            send_sem=rs_send.at[k - 1],
            recv_sem=rs_recv.at[k - 1],
            device_id=(me_a, lax.rem(me_b + k, nb)),
            device_id_type=MESH,
        )

    @pl.when(me_b > 0)
    def _():
        pass_on(nb - me_b, early).start()

    low_bits = (low - 1).bit_length()
    part_bits = (parts - 1).bit_length()
    target = bt_v[...]
    upper = target >> low_bits
    high_v[...] = ((upper & (parts - 1)) * nb + (upper >> part_bits)).astype(f32)
    low_v[...] = (target & (low - 1)).astype(f32)
    low_ids = lax.broadcasted_iota(jnp.int32, (low, LANES), 0).astype(f32).astype(bf16)
    high_ids = lax.broadcasted_iota(jnp.int32, (high, LANES), 0).astype(f32).astype(bf16)
    one, zero = jnp.ones((), bf16), jnp.zeros((), bf16)

    @pl.loop(0, slots // few)
    def _(i):
        for r in range(few):
            row = i * few + r
            where = pl.ds(pl.multiple_of(row * LANES, LANES), LANES)
            wanted = jnp.broadcast_to(low_v[pl.ds(row, 1), :].astype(bf16), (low, LANES))
            hot[:, where] = jnp.where(low_ids == wanted, one, zero)
            wanted = jnp.broadcast_to(high_v[pl.ds(row, 1), :].astype(bf16), (high, LANES))
            group[:, where] = jnp.where(high_ids == wanted, one, zero)

    turn = slots // 2 if slots % 2 == 0 else slots

    def step(i, total):
        lhs = []
        for r in range(turn):
            row = i * turn + r
            match = group[:, pl.ds(pl.multiple_of(row * LANES, LANES), LANES)]
            lhs.append(
                jnp.concatenate(
                    [
                        match * jnp.broadcast_to(vals[m, pl.ds(row, 1), :], (high, LANES)).astype(bf16)
                        for m in range(2 * rows)
                    ],
                    axis=0,
                )
            )
        width = turn * LANES
        part = hot[:, pl.ds(pl.multiple_of(i * width, LANES), width)]
        return total + dot(jnp.concatenate(lhs, axis=1), part, NT)

    total = lax.fori_loop(0, slots // turn, step, jnp.zeros((2 * rows * high, low), f32))
    for a in range(rows):
        both = total[a * high : (a + 1) * high] + total[(rows + a) * high : (rows + a + 1) * high]
        send[:, a, :] = jnp.concatenate([both[i * nb : (i + 1) * nb] for i in range(parts)], axis=1)


    @pl.when(me_b < nb - 1)
    def _():
        pl.semaphore_wait(ready, nb - 1 - me_b)

    for k in range(1, nb):
        to = lax.rem(me_b + k, nb)

        @pl.when(to > 0)
        def _():
            pass_on(k, send.at[to]).start()

    weight = jnp.sum(counts_v[...] * h_v[...], axis=1, keepdims=True)
    c = jnp.concatenate([slab[i] for i in range(na)], axis=0)
    local = [jnp.sum(weight[a * alphas : (a + 1) * alphas] * c, axis=0, keepdims=True) for a in range(rows)]
    result = jnp.concatenate(local, axis=0) + send[me_b]
    for copy in gathers:
        copy.wait_send()
    for k in range(1, nb):
        pass_on(k, early).wait_send()
    for k in range(nb - 1, 0, -1):
        pass_on(k, early).wait_recv()
        result = result + recv[k - 1]
    out[...] = result


def solution(mesh):
    na, nb = mesh.shape["alpha"], mesh.shape["beta"]

    def per_device(coeffs, a_target, a_pair, a_sign, b_target, b_pair, b_sign, integrals, one_body):
        rows, cols = coeffs.shape
        slots = a_target.shape[1]
        norb = one_body.shape[0]
        wide = pl.cdiv(norb * norb, LANES) * LANES
        assert cols == LANES
        low = cols // 2
        small = cols // 4
        high = nb * (cols // low)
        i32, f32, bf16 = jnp.int32, jnp.float32, jnp.bfloat16
        pairs = rows * na * rows
        return pl.pallas_call(
            functools.partial(kernel, na, nb, low, small),
            out_shape=pltpu.VMEM((rows, cols), f32),
            in_specs=[pl.BlockSpec(memory_space=pl.ANY)] * 9,
            out_specs=pl.BlockSpec(memory_space=pltpu.VMEM),
            scratch_shapes=[
                pltpu.VMEM(a_target.shape, i32),
                pltpu.VMEM(a_pair.shape, i32),
                pltpu.VMEM(a_sign.shape, i32),
                pltpu.VMEM(b_target.shape[::-1], i32),
                pltpu.VMEM(b_pair.shape[::-1], i32),
                pltpu.VMEM(b_sign.shape[::-1], i32),
                pltpu.VMEM(integrals.shape, f32),
                pltpu.VMEM(one_body.shape, f32),
                pltpu.VMEM((na, rows, cols), f32),
                pltpu.VMEM((pairs, wide), f32),
                pltpu.VMEM((pairs, wide), f32),
                pltpu.VMEM((1, wide), f32),
                pltpu.VMEM((slots, LANES), f32),
                pltpu.VMEM((slots, LANES), f32),
                pltpu.VMEM((pairs, slots, LANES), f32),
                pltpu.VMEM((2 * rows, slots, LANES), f32),
                pltpu.VMEM((low, slots * LANES), bf16),
                pltpu.VMEM((high, slots * LANES), bf16),
                pltpu.VMEM((slots, LANES), f32),
                pltpu.VMEM((slots, LANES), f32),
                pltpu.VMEM((small, slots * LANES), bf16),
                pltpu.VMEM((2 * rows * (cols // small), slots * LANES), bf16),
                pltpu.VMEM((rows, cols), f32),
                pltpu.VMEM((nb, rows, cols), f32),
                pltpu.VMEM((nb - 1, rows, cols), f32),
                pltpu.SemaphoreType.DMA((9,)),
                pltpu.SemaphoreType.DMA((na - 1,)),
                pltpu.SemaphoreType.DMA((na - 1,)),
                pltpu.SemaphoreType.DMA((nb - 1,)),
                pltpu.SemaphoreType.DMA((nb - 1,)),
                pltpu.SemaphoreType.REGULAR,
            ],
            compiler_params=pltpu.CompilerParams(collective_id=0, has_side_effects=True),
        )(coeffs, a_target, a_pair, a_sign, b_target.T, b_pair.T, b_sign.T, integrals, one_body)

    placed = (
        P("alpha", "beta"),
        P("alpha", None),
        P("alpha", None),
        P("alpha", None),
        P("beta", None),
        P("beta", None),
        P("beta", None),
        P(),
        P(),
    )
    return jax.shard_map(
        per_device, mesh=mesh, in_specs=placed, out_specs=P("alpha", "beta"), check_vma=False
    )
```

```python
import functools

import jax
import jax.numpy as jnp
from jax import lax
from jax.experimental import pallas as pl
from jax.experimental.pallas import tpu as pltpu
from jax.sharding import PartitionSpec as P

MESH = pl.DeviceIdType.MESH
LANES = 128
SUB = 8
NT = (((1,), (1,)), ((), ()))
NN = (((1,), (0,)), ((), ()))


def dot(a, b, dims=NN):
    return lax.dot_general(a, b, dims, preferred_element_type=jnp.float32)


def split(x):
    top = x.astype(jnp.bfloat16).astype(jnp.float32)
    return top, x - top


def divider(n, limit):
    s = 16
    m = (1 << s) // n + 1
    assert all((x * m) >> s == x // n for x in range(limit)) and limit * m < 2**31
    return m, s


def kernel(
    na,
    nb,
    low,
    small,
    coeffs,
    a_target,
    a_pair,
    a_sign,
    b_target,
    b_pair,
    b_sign,
    integrals,
    one_body,
    out,
    at_v,
    ap_v,
    as_v,
    bt_v,
    bp_v,
    bs_v,
    int_v,
    ob_v,
    slab,
    g_v,
    counts_v,
    h_v,
    high_v,
    low_v,
    picked,
    vals,
    hot,
    group,
    first_v,
    small_v,
    small_hot,
    small_group,
    early,
    send,
    recv,
    load_sem,
    ag_send,
    ag_recv,
    rs_send,
    rs_recv,
    ready,
):
    rows, cols = coeffs.shape
    slots = a_target.shape[1]
    norb = one_body.shape[0]
    npairs = norb * norb
    wide = g_v.shape[1]
    alphas = na * rows
    parts = cols // low
    high = parts * nb
    me_a = lax.axis_index("alpha")
    me_b = lax.axis_index("beta")
    f32, bf16 = jnp.float32, jnp.bfloat16

    loads = [
        pltpu.make_async_copy(src, dst, load_sem.at[i])
        for i, (src, dst) in enumerate(
            (
                (coeffs, slab.at[me_a]),
                (a_target, at_v),
                (a_pair, ap_v),
                (a_sign, as_v),
                (b_target, bt_v),
                (one_body, ob_v),
                (b_pair, bp_v),
                (b_sign, bs_v),
                (integrals, int_v),
            )
        )
    ]
    barrier = pltpu.get_barrier_semaphore()
    for k in range(1, na):
        pl.semaphore_signal(barrier, inc=1, device_id=(lax.rem(me_a + k, na), me_b), device_id_type=MESH)

    @pl.loop(me_b + 1, nb)
    def _(peer):
        pl.semaphore_signal(barrier, inc=1, device_id=(me_a, peer), device_id_type=MESH)

    for load in loads:
        load.start()
    gathers = [
        pltpu.make_async_remote_copy(
            src_ref=slab.at[me_a],
            dst_ref=slab.at[me_a],
            send_sem=ag_send.at[k - 1],
            recv_sem=ag_recv.at[k - 1],
            device_id=(lax.rem(me_a + k, na), me_b),
            device_id_type=MESH,
        )
        for k in range(1, na)
    ]

    def meet():
        pl.semaphore_wait(barrier, na - 1 + me_b)
        loads[0].wait()
        for copy in gathers:
            copy.start()

        @pl.loop(0, me_b)
        def _(peer):
            pl.semaphore_signal(ready, inc=1, device_id=(me_a, peer), device_id_type=MESH)

    far = 2 * me_a >= na

    @pl.when(far)
    def _():
        meet()

    sets = LANES // small
    few = next(n for n in range(12, 0, -1) if slots % n == 0)
    one, zero = jnp.ones((), bf16), jnp.zeros((), bf16)

    def prepare():
        for i in range(1, 5):
            loads[i].wait()
        pair_ids = lax.broadcasted_iota(jnp.int32, (wide, slots), 0)
        string_ids = lax.broadcasted_iota(jnp.int32, (alphas, slots), 0)
        for a in range(rows):
            hits = jnp.where(pair_ids == ap_v[a : a + 1, :], 1.0, 0.0).astype(bf16)
            reach = jnp.where(string_ids == at_v[a : a + 1, :], as_v[a : a + 1, :].astype(f32), 0.0)
            counts_v[a * alphas : (a + 1) * alphas, :] = dot(reach.astype(bf16), hits, NT)

        target = bt_v[...]
        one, zero = jnp.ones((), bf16), jnp.zeros((), bf16)
        sets = LANES // small
        small_bits = (small - 1).bit_length()
        first_v[...] = (target >> small_bits).astype(f32)
        small_v[...] = (target & (small - 1)).astype(f32)
        small_ids = lax.broadcasted_iota(jnp.int32, (small, LANES), 0).astype(f32).astype(bf16)
        set_ids = (lax.broadcasted_iota(jnp.int32, (2 * rows * sets, LANES), 0) & (sets - 1)).astype(f32).astype(bf16)

        def spots(row):
            where = pl.ds(pl.multiple_of(row * LANES, LANES), LANES)
            wanted = jnp.broadcast_to(small_v[pl.ds(row, 1), :].astype(bf16), (small, LANES))
            small_hot[:, where] = jnp.where(small_ids == wanted, one, zero)
            wanted = jnp.broadcast_to(first_v[pl.ds(row, 1), :].astype(bf16), (2 * rows * sets, LANES))
            small_group[:, where] = jnp.where(set_ids == wanted, one, zero)

        @pl.loop(0, slots // few)
        def _(i):
            for r in range(few):
                spots(i * few + r)

        @pl.when(jnp.logical_not(far))
        def _():
            meet()

        for i in range(5, 9):
            loads[i].wait()
        counts = counts_v[...]
        mul, shift = divider(norb, wide)
        q = lax.broadcasted_iota(jnp.int32, (norb, wide), 1)
        q_row = (q * mul) >> shift
        q_col = q - q_row * norb
        orbital = lax.broadcasted_iota(jnp.int32, (norb, wide), 0)
        spread_h = lax.dot_general(
            ob_v[...],
            jnp.where(q_col == orbital, 1.0, 0.0),
            NN,
            precision=lax.Precision.HIGHEST,
            preferred_element_type=f32,
        )
        h = jnp.sum(jnp.where(q_row == orbital, spread_h, 0.0), axis=0, keepdims=True)
        h_v[...] = h
        exact = counts[:, :npairs].astype(bf16)
        int_top, int_rest = split(int_v[...])
        g_v[...] = jnp.zeros_like(g_v)
        g_v[:, :npairs] = dot(exact, int_top.astype(bf16)) + dot(exact, int_rest.astype(bf16))
        line = lax.broadcasted_iota(jnp.int32, (rows * alphas, wide), 0)
        own = line == me_a * rows
        for a in range(1, rows):
            own = own | (line == a * alphas + me_a * rows + a)
        g_v[...] = g_v[...] + jnp.where(own, h, 0.0)

        def pick(lower, count):
            here = pl.ds(lower, count)
            pair = bp_v[here, :]
            row = (pair * mul) >> shift
            swapped = (pair - row * norb) * norb + row
            lane = swapped & (LANES - 1)
            piece = swapped >> (LANES.bit_length() - 1)
            sign = bs_v[here, :].astype(f32)
            for r in range(rows * alphas):
                value = None
                for i in range(wide // LANES):
                    table = jnp.broadcast_to(g_v[r : r + 1, i * LANES : (i + 1) * LANES], (count, LANES))
                    found = jnp.take_along_axis(table, lane, axis=1, mode="promise_in_bounds")
                    value = found if value is None else jnp.where(piece == i, found, value)
                picked[r, here, :] = value * sign

        blocks = slots // SUB
        several = next(n for n in (16, 8, 3, 2, 1) if blocks % n == 0)

        @pl.loop(0, blocks // several)
        def _(i):
            for n in range(several):
                pick(pl.multiple_of((i * several + n) * SUB, SUB), SUB)

        if slots % SUB:
            pick(blocks * SUB, slots % SUB)

        late = lax.rem(me_a + na // 2, na)
        for k in range(1, na):
            if k != na // 2:
                gathers[k - 1].wait_recv()

        def weigh(here, a, first, count):
            value = None
            for n in range(first, first + count):
                which = lax.rem(late + n, na)
                block = slab[which]
                for r in range(rows):
                    term = picked[a * alphas + which * rows + r, here, :] * block[r : r + 1]
                    value = term if value is None else value + term
            return value

        @pl.loop(0, blocks // 4)
        def _(i):
            for n in range(4):
                here = pl.ds(pl.multiple_of((i * 4 + n) * SUB, SUB), SUB)
                for a in range(rows):
                    vals[a, here, :] = weigh(here, a, 1, na - 1)

        tail = pl.ds(blocks // 4 * 4 * SUB, slots - blocks // 4 * 4 * SUB)
        for a in range(rows):
            vals[a, tail, :] = weigh(tail, a, 1, na - 1)
        gathers[na // 2 - 1].wait_recv()
        for lower in range(0, slots, SUB):
            here = pl.ds(lower, min(SUB, slots - lower))
            for a in range(rows):
                top, rest = split(vals[a, here, :] + weigh(here, a, 0, 1))
                vals[a, here, :] = top
                vals[rows + a, here, :] = rest

    @pl.loop(0, 2)
    def _(i):
        @pl.when(i == 1)
        def _():
            prepare()

        lhs = []
        for row in range(slots):
            match = small_group[:, row * LANES : (row + 1) * LANES]
            value = [jnp.broadcast_to(vals[m, row : row + 1, :], (sets, LANES)) for m in range(2 * rows)]
            lhs.append(match * jnp.concatenate(value, axis=0).astype(bf16))
        total = dot(jnp.concatenate(lhs, axis=1), small_hot[...], NT)
        both = total[: rows * sets] + total[rows * sets :]
        for a in range(rows):
            early[a : a + 1, :] = jnp.concatenate([both[a * sets + n : a * sets + n + 1] for n in range(sets)], axis=1)

    def pass_on(k, source):
        return pltpu.make_async_remote_copy(
            src_ref=source,
            dst_ref=recv.at[k - 1],
            send_sem=rs_send.at[k - 1],
            recv_sem=rs_recv.at[k - 1],
            device_id=(me_a, lax.rem(me_b + k, nb)),
            device_id_type=MESH,
        )

    @pl.when(me_b > 0)
    def _():
        pass_on(nb - me_b, early).start()

    low_bits = (low - 1).bit_length()
    part_bits = (parts - 1).bit_length()
    target = bt_v[...]
    upper = target >> low_bits
    high_v[...] = ((upper & (parts - 1)) * nb + (upper >> part_bits)).astype(f32)
    low_v[...] = (target & (low - 1)).astype(f32)
    low_ids = lax.broadcasted_iota(jnp.int32, (low, LANES), 0).astype(f32).astype(bf16)
    high_ids = lax.broadcasted_iota(jnp.int32, (high, LANES), 0).astype(f32).astype(bf16)
    one, zero = jnp.ones((), bf16), jnp.zeros((), bf16)

    @pl.loop(0, slots // few)
    def _(i):
        for r in range(few):
            row = i * few + r
            where = pl.ds(pl.multiple_of(row * LANES, LANES), LANES)
            wanted = jnp.broadcast_to(low_v[pl.ds(row, 1), :].astype(bf16), (low, LANES))
            hot[:, where] = jnp.where(low_ids == wanted, one, zero)
            wanted = jnp.broadcast_to(high_v[pl.ds(row, 1), :].astype(bf16), (high, LANES))
            group[:, where] = jnp.where(high_ids == wanted, one, zero)

    turn = slots // 2 if slots % 2 == 0 else slots

    def step(i, total):
        lhs = []
        for r in range(turn):
            row = i * turn + r
            match = group[:, pl.ds(pl.multiple_of(row * LANES, LANES), LANES)]
            lhs.append(
                jnp.concatenate(
                    [
                        match * jnp.broadcast_to(vals[m, pl.ds(row, 1), :], (high, LANES)).astype(bf16)
                        for m in range(2 * rows)
                    ],
                    axis=0,
                )
            )
        width = turn * LANES
        part = hot[:, pl.ds(pl.multiple_of(i * width, LANES), width)]
        return total + dot(jnp.concatenate(lhs, axis=1), part, NT)

    total = lax.fori_loop(0, slots // turn, step, jnp.zeros((2 * rows * high, low), f32))
    for a in range(rows):
        both = total[a * high : (a + 1) * high] + total[(rows + a) * high : (rows + a + 1) * high]
        send[:, a, :] = jnp.concatenate([both[i * nb : (i + 1) * nb] for i in range(parts)], axis=1)


    @pl.when(me_b < nb - 1)
    def _():
        pl.semaphore_wait(ready, nb - 1 - me_b)

    for k in range(1, nb):
        to = lax.rem(me_b + k, nb)

        @pl.when(to > 0)
        def _():
            pass_on(k, send.at[to]).start()

    weight = jnp.sum(counts_v[...] * h_v[...], axis=1, keepdims=True)
    c = jnp.concatenate([slab[i] for i in range(na)], axis=0)
    local = [jnp.sum(weight[a * alphas : (a + 1) * alphas] * c, axis=0, keepdims=True) for a in range(rows)]
    result = jnp.concatenate(local, axis=0) + send[me_b]
    for copy in gathers:
        copy.wait_send()
    for k in range(1, nb):
        pass_on(k, early).wait_send()
    for k in range(nb - 1, 0, -1):
        pass_on(k, early).wait_recv()
        result = result + recv[k - 1]
    out[...] = result


def solution(mesh):
    na, nb = mesh.shape["alpha"], mesh.shape["beta"]

    def per_device(coeffs, a_target, a_pair, a_sign, b_target, b_pair, b_sign, integrals, one_body):
        rows, cols = coeffs.shape
        slots = a_target.shape[1]
        norb = one_body.shape[0]
        wide = pl.cdiv(norb * norb, LANES) * LANES
        assert cols == LANES
        low = cols // 2
        small = cols // 4
        high = nb * (cols // low)
        i32, f32, bf16 = jnp.int32, jnp.float32, jnp.bfloat16
        pairs = rows * na * rows
        return pl.pallas_call(
            functools.partial(kernel, na, nb, low, small),
            out_shape=pltpu.VMEM((rows, cols), f32),
            in_specs=[pl.BlockSpec(memory_space=pl.ANY)] * 9,
            out_specs=pl.BlockSpec(memory_space=pltpu.VMEM),
            scratch_shapes=[
                pltpu.VMEM(a_target.shape, i32),
                pltpu.VMEM(a_pair.shape, i32),
                pltpu.VMEM(a_sign.shape, i32),
                pltpu.VMEM(b_target.shape[::-1], i32),
                pltpu.VMEM(b_pair.shape[::-1], i32),
                pltpu.VMEM(b_sign.shape[::-1], i32),
                pltpu.VMEM(integrals.shape, f32),
                pltpu.VMEM(one_body.shape, f32),
                pltpu.VMEM((na, rows, cols), f32),
                pltpu.VMEM((pairs, wide), f32),
                pltpu.VMEM((pairs, wide), f32),
                pltpu.VMEM((1, wide), f32),
                pltpu.VMEM((slots, LANES), f32),
                pltpu.VMEM((slots, LANES), f32),
                pltpu.VMEM((pairs, slots, LANES), f32),
                pltpu.VMEM((2 * rows, slots, LANES), f32),
                pltpu.VMEM((low, slots * LANES), bf16),
                pltpu.VMEM((high, slots * LANES), bf16),
                pltpu.VMEM((slots, LANES), f32),
                pltpu.VMEM((slots, LANES), f32),
                pltpu.VMEM((small, slots * LANES), bf16),
                pltpu.VMEM((2 * rows * (cols // small), slots * LANES), bf16),
                pltpu.VMEM((rows, cols), f32),
                pltpu.VMEM((nb, rows, cols), f32),
                pltpu.VMEM((nb - 1, rows, cols), f32),
                pltpu.SemaphoreType.DMA((9,)),
                pltpu.SemaphoreType.DMA((na - 1,)),
                pltpu.SemaphoreType.DMA((na - 1,)),
                pltpu.SemaphoreType.DMA((nb - 1,)),
                pltpu.SemaphoreType.DMA((nb - 1,)),
                pltpu.SemaphoreType.REGULAR,
            ],
            compiler_params=pltpu.CompilerParams(collective_id=0, has_side_effects=True),
        )(coeffs, a_target, a_pair, a_sign, b_target.T, b_pair.T, b_sign.T, integrals, one_body)

    placed = (
        P("alpha", "beta"),
        P("alpha", None),
        P("alpha", None),
        P("alpha", None),
        P("beta", None),
        P("beta", None),
        P("beta", None),
        P(),
        P(),
    )
    return jax.shard_map(
        per_device, mesh=mesh, in_specs=placed, out_specs=P("alpha", "beta"), check_vma=False
    )
```

```python
import functools

import jax
import jax.numpy as jnp
from jax import lax
from jax.experimental import pallas as pl
from jax.experimental.pallas import tpu as pltpu
from jax.sharding import PartitionSpec as P

MESH = pl.DeviceIdType.MESH
LANES = 128
SUB = 8
NT = (((1,), (1,)), ((), ()))
NN = (((1,), (0,)), ((), ()))


def dot(a, b, dims=NN):
    return lax.dot_general(a, b, dims, preferred_element_type=jnp.float32)


def split(x):
    top = x.astype(jnp.bfloat16).astype(jnp.float32)
    return top, x - top


def divider(n, limit):
    s = 16
    m = (1 << s) // n + 1
    assert all((x * m) >> s == x // n for x in range(limit)) and limit * m < 2**31
    return m, s


def kernel(
    na,
    nb,
    low,
    small,
    coeffs,
    a_target,
    a_pair,
    a_sign,
    b_target,
    b_pair,
    b_sign,
    integrals,
    one_body,
    out,
    at_v,
    ap_v,
    as_v,
    bt_v,
    bp_v,
    bs_v,
    int_v,
    ob_v,
    slab,
    g_v,
    counts_v,
    h_v,
    high_v,
    low_v,
    picked,
    vals,
    hot,
    group,
    first_v,
    small_v,
    small_hot,
    small_group,
    early,
    send,
    recv,
    load_sem,
    ag_send,
    ag_recv,
    rs_send,
    rs_recv,
    ready,
):
    rows, cols = coeffs.shape
    slots = a_target.shape[1]
    norb = one_body.shape[0]
    npairs = norb * norb
    wide = g_v.shape[1]
    alphas = na * rows
    parts = cols // low
    high = parts * nb
    me_a = lax.axis_index("alpha")
    me_b = lax.axis_index("beta")
    f32, bf16 = jnp.float32, jnp.bfloat16

    loads = [
        pltpu.make_async_copy(src, dst, load_sem.at[i])
        for i, (src, dst) in enumerate(
            (
                (coeffs, slab.at[me_a]),
                (a_target, at_v),
                (a_pair, ap_v),
                (a_sign, as_v),
                (b_target, bt_v),
                (one_body, ob_v),
                (b_pair, bp_v),
                (b_sign, bs_v),
                (integrals, int_v),
            )
        )
    ]
    barrier = pltpu.get_barrier_semaphore()
    order = sorted(range(1, na), key=lambda k: k != na // 2)
    for k in order:
        pl.semaphore_signal(barrier, inc=1, device_id=(lax.rem(me_a + k, na), me_b), device_id_type=MESH)

    @pl.loop(me_b + 1, nb)
    def _(peer):
        pl.semaphore_signal(barrier, inc=1, device_id=(me_a, peer), device_id_type=MESH)

    for load in loads:
        load.start()
    gathers = [
        pltpu.make_async_remote_copy(
            src_ref=slab.at[me_a],
            dst_ref=slab.at[me_a],
            send_sem=ag_send.at[k - 1],
            recv_sem=ag_recv.at[k - 1],
            device_id=(lax.rem(me_a + k, na), me_b),
            device_id_type=MESH,
        )
        for k in range(1, na)
    ]

    def meet():
        pl.semaphore_wait(barrier, na - 1 + me_b)
        loads[0].wait()
        for k in order:
            gathers[k - 1].start()

        @pl.loop(0, me_b)
        def _(peer):
            pl.semaphore_signal(ready, inc=1, device_id=(me_a, peer), device_id_type=MESH)

    far = 2 * me_a >= na

    @pl.when(far)
    def _():
        meet()

    sets = LANES // small
    few = next(n for n in range(12, 0, -1) if slots % n == 0)
    one, zero = jnp.ones((), bf16), jnp.zeros((), bf16)

    def prepare():
        for i in range(1, 5):
            loads[i].wait()
        pair_ids = lax.broadcasted_iota(jnp.int32, (wide, slots), 0)
        string_ids = lax.broadcasted_iota(jnp.int32, (alphas, slots), 0)
        for a in range(rows):
            hits = jnp.where(pair_ids == ap_v[a : a + 1, :], 1.0, 0.0).astype(bf16)
            reach = jnp.where(string_ids == at_v[a : a + 1, :], as_v[a : a + 1, :].astype(f32), 0.0)
            counts_v[a * alphas : (a + 1) * alphas, :] = dot(reach.astype(bf16), hits, NT)

        target = bt_v[...]
        one, zero = jnp.ones((), bf16), jnp.zeros((), bf16)
        sets = LANES // small
        small_bits = (small - 1).bit_length()
        first_v[...] = (target >> small_bits).astype(f32)
        small_v[...] = (target & (small - 1)).astype(f32)
        small_ids = lax.broadcasted_iota(jnp.int32, (small, LANES), 0).astype(f32).astype(bf16)
        set_ids = (lax.broadcasted_iota(jnp.int32, (2 * rows * sets, LANES), 0) & (sets - 1)).astype(f32).astype(bf16)

        def spots(row):
            where = pl.ds(pl.multiple_of(row * LANES, LANES), LANES)
            wanted = jnp.broadcast_to(small_v[pl.ds(row, 1), :].astype(bf16), (small, LANES))
            small_hot[:, where] = jnp.where(small_ids == wanted, one, zero)
            wanted = jnp.broadcast_to(first_v[pl.ds(row, 1), :].astype(bf16), (2 * rows * sets, LANES))
            small_group[:, where] = jnp.where(set_ids == wanted, one, zero)

        @pl.loop(0, slots // few)
        def _(i):
            for r in range(few):
                spots(i * few + r)

        @pl.when(jnp.logical_not(far))
        def _():
            meet()

        for i in range(5, 9):
            loads[i].wait()
        counts = counts_v[...]
        mul, shift = divider(norb, wide)
        q = lax.broadcasted_iota(jnp.int32, (norb, wide), 1)
        q_row = (q * mul) >> shift
        q_col = q - q_row * norb
        orbital = lax.broadcasted_iota(jnp.int32, (norb, wide), 0)
        spread_h = lax.dot_general(
            ob_v[...],
            jnp.where(q_col == orbital, 1.0, 0.0),
            NN,
            precision=lax.Precision.HIGHEST,
            preferred_element_type=f32,
        )
        h = jnp.sum(jnp.where(q_row == orbital, spread_h, 0.0), axis=0, keepdims=True)
        h_v[...] = h
        exact = counts[:, :npairs].astype(bf16)
        int_top, int_rest = split(int_v[...])
        g_v[...] = jnp.zeros_like(g_v)
        g_v[:, :npairs] = dot(exact, int_top.astype(bf16)) + dot(exact, int_rest.astype(bf16))
        line = lax.broadcasted_iota(jnp.int32, (rows * alphas, wide), 0)
        own = line == me_a * rows
        for a in range(1, rows):
            own = own | (line == a * alphas + me_a * rows + a)
        g_v[...] = g_v[...] + jnp.where(own, h, 0.0)

        def pick(lower, count):
            here = pl.ds(lower, count)
            pair = bp_v[here, :]
            row = (pair * mul) >> shift
            swapped = (pair - row * norb) * norb + row
            lane = swapped & (LANES - 1)
            piece = swapped >> (LANES.bit_length() - 1)
            sign = bs_v[here, :].astype(f32)
            for r in range(rows * alphas):
                value = None
                for i in range(wide // LANES):
                    table = jnp.broadcast_to(g_v[r : r + 1, i * LANES : (i + 1) * LANES], (count, LANES))
                    found = jnp.take_along_axis(table, lane, axis=1, mode="promise_in_bounds")
                    value = found if value is None else jnp.where(piece == i, found, value)
                picked[r, here, :] = value * sign

        blocks = slots // SUB
        several = next(n for n in (16, 8, 3, 2, 1) if blocks % n == 0)

        @pl.loop(0, blocks // several)
        def _(i):
            for n in range(several):
                pick(pl.multiple_of((i * several + n) * SUB, SUB), SUB)

        if slots % SUB:
            pick(blocks * SUB, slots % SUB)

        for k in sorted(range(1, na), key=lambda k: k == na // 2):
            gathers[k - 1].wait_recv()
        c = jnp.concatenate([slab[i] for i in range(na)], axis=0)
        for lower in range(0, slots, SUB):
            upper = min(lower + SUB, slots)
            for a in range(rows):
                value = None
                for i in range(alphas):
                    term = picked[a * alphas + i, lower:upper, :] * c[i : i + 1]
                    value = term if value is None else value + term
                top, rest = split(value)
                vals[a, lower:upper, :] = top
                vals[rows + a, lower:upper, :] = rest


    @pl.loop(0, 2)
    def _(i):
        @pl.when(i == 1)
        def _():
            prepare()

        lhs = []
        for row in range(slots):
            match = small_group[:, row * LANES : (row + 1) * LANES]
            value = [jnp.broadcast_to(vals[m, row : row + 1, :], (sets, LANES)) for m in range(2 * rows)]
            lhs.append(match * jnp.concatenate(value, axis=0).astype(bf16))
        total = dot(jnp.concatenate(lhs, axis=1), small_hot[...], NT)
        both = total[: rows * sets] + total[rows * sets :]
        for a in range(rows):
            early[a : a + 1, :] = jnp.concatenate([both[a * sets + n : a * sets + n + 1] for n in range(sets)], axis=1)

    def pass_on(k, source):
        return pltpu.make_async_remote_copy(
            src_ref=source,
            dst_ref=recv.at[k - 1],
            send_sem=rs_send.at[k - 1],
            recv_sem=rs_recv.at[k - 1],
            device_id=(me_a, lax.rem(me_b + k, nb)),
            device_id_type=MESH,
        )

    @pl.when(me_b > 0)
    def _():
        pass_on(nb - me_b, early).start()

    low_bits = (low - 1).bit_length()
    part_bits = (parts - 1).bit_length()
    target = bt_v[...]
    upper = target >> low_bits
    high_v[...] = ((upper & (parts - 1)) * nb + (upper >> part_bits)).astype(f32)
    low_v[...] = (target & (low - 1)).astype(f32)
    low_ids = lax.broadcasted_iota(jnp.int32, (low, LANES), 0).astype(f32).astype(bf16)
    high_ids = lax.broadcasted_iota(jnp.int32, (high, LANES), 0).astype(f32).astype(bf16)
    one, zero = jnp.ones((), bf16), jnp.zeros((), bf16)

    @pl.loop(0, slots // few)
    def _(i):
        for r in range(few):
            row = i * few + r
            where = pl.ds(pl.multiple_of(row * LANES, LANES), LANES)
            wanted = jnp.broadcast_to(low_v[pl.ds(row, 1), :].astype(bf16), (low, LANES))
            hot[:, where] = jnp.where(low_ids == wanted, one, zero)
            wanted = jnp.broadcast_to(high_v[pl.ds(row, 1), :].astype(bf16), (high, LANES))
            group[:, where] = jnp.where(high_ids == wanted, one, zero)

    turn = slots // 2 if slots % 2 == 0 else slots

    def step(i, total):
        lhs = []
        for r in range(turn):
            row = i * turn + r
            match = group[:, pl.ds(pl.multiple_of(row * LANES, LANES), LANES)]
            lhs.append(
                jnp.concatenate(
                    [
                        match * jnp.broadcast_to(vals[m, pl.ds(row, 1), :], (high, LANES)).astype(bf16)
                        for m in range(2 * rows)
                    ],
                    axis=0,
                )
            )
        width = turn * LANES
        part = hot[:, pl.ds(pl.multiple_of(i * width, LANES), width)]
        return total + dot(jnp.concatenate(lhs, axis=1), part, NT)

    total = lax.fori_loop(0, slots // turn, step, jnp.zeros((2 * rows * high, low), f32))
    for a in range(rows):
        both = total[a * high : (a + 1) * high] + total[(rows + a) * high : (rows + a + 1) * high]
        send[:, a, :] = jnp.concatenate([both[i * nb : (i + 1) * nb] for i in range(parts)], axis=1)


    @pl.when(me_b < nb - 1)
    def _():
        pl.semaphore_wait(ready, nb - 1 - me_b)

    for k in range(1, nb):
        to = lax.rem(me_b + k, nb)

        @pl.when(to > 0)
        def _():
            pass_on(k, send.at[to]).start()

    weight = jnp.sum(counts_v[...] * h_v[...], axis=1, keepdims=True)
    c = jnp.concatenate([slab[i] for i in range(na)], axis=0)
    local = [jnp.sum(weight[a * alphas : (a + 1) * alphas] * c, axis=0, keepdims=True) for a in range(rows)]
    result = jnp.concatenate(local, axis=0) + send[me_b]
    for copy in gathers:
        copy.wait_send()
    for k in range(1, nb):
        pass_on(k, early).wait_send()
    for k in range(nb - 1, 0, -1):
        pass_on(k, early).wait_recv()
        result = result + recv[k - 1]
    out[...] = result


def solution(mesh):
    na, nb = mesh.shape["alpha"], mesh.shape["beta"]

    def per_device(coeffs, a_target, a_pair, a_sign, b_target, b_pair, b_sign, integrals, one_body):
        rows, cols = coeffs.shape
        slots = a_target.shape[1]
        norb = one_body.shape[0]
        wide = pl.cdiv(norb * norb, LANES) * LANES
        assert cols == LANES
        low = cols // 2
        small = cols // 4
        high = nb * (cols // low)
        i32, f32, bf16 = jnp.int32, jnp.float32, jnp.bfloat16
        pairs = rows * na * rows
        return pl.pallas_call(
            functools.partial(kernel, na, nb, low, small),
            out_shape=pltpu.VMEM((rows, cols), f32),
            in_specs=[pl.BlockSpec(memory_space=pl.ANY)] * 9,
            out_specs=pl.BlockSpec(memory_space=pltpu.VMEM),
            scratch_shapes=[
                pltpu.VMEM(a_target.shape, i32),
                pltpu.VMEM(a_pair.shape, i32),
                pltpu.VMEM(a_sign.shape, i32),
                pltpu.VMEM(b_target.shape[::-1], i32),
                pltpu.VMEM(b_pair.shape[::-1], i32),
                pltpu.VMEM(b_sign.shape[::-1], i32),
                pltpu.VMEM(integrals.shape, f32),
                pltpu.VMEM(one_body.shape, f32),
                pltpu.VMEM((na, rows, cols), f32),
                pltpu.VMEM((pairs, wide), f32),
                pltpu.VMEM((pairs, wide), f32),
                pltpu.VMEM((1, wide), f32),
                pltpu.VMEM((slots, LANES), f32),
                pltpu.VMEM((slots, LANES), f32),
                pltpu.VMEM((pairs, slots, LANES), f32),
                pltpu.VMEM((2 * rows, slots, LANES), f32),
                pltpu.VMEM((low, slots * LANES), bf16),
                pltpu.VMEM((high, slots * LANES), bf16),
                pltpu.VMEM((slots, LANES), f32),
                pltpu.VMEM((slots, LANES), f32),
                pltpu.VMEM((small, slots * LANES), bf16),
                pltpu.VMEM((2 * rows * (cols // small), slots * LANES), bf16),
                pltpu.VMEM((rows, cols), f32),
                pltpu.VMEM((nb, rows, cols), f32),
                pltpu.VMEM((nb - 1, rows, cols), f32),
                pltpu.SemaphoreType.DMA((9,)),
                pltpu.SemaphoreType.DMA((na - 1,)),
                pltpu.SemaphoreType.DMA((na - 1,)),
                pltpu.SemaphoreType.DMA((nb - 1,)),
                pltpu.SemaphoreType.DMA((nb - 1,)),
                pltpu.SemaphoreType.REGULAR,
            ],
            compiler_params=pltpu.CompilerParams(collective_id=0, has_side_effects=True),
        )(coeffs, a_target, a_pair, a_sign, b_target.T, b_pair.T, b_sign.T, integrals, one_body)

    placed = (
        P("alpha", "beta"),
        P("alpha", None),
        P("alpha", None),
        P("alpha", None),
        P("beta", None),
        P("beta", None),
        P("beta", None),
        P(),
        P(),
    )
    return jax.shard_map(
        per_device, mesh=mesh, in_specs=placed, out_specs=P("alpha", "beta"), check_vma=False
    )
```
